512 devices in a mesh: row: 32 (over x, z_lo, core), col: 16 (over y, z_hi).
Axes of the slice: x: 4, y: 4, z: 16 (z_hi: 4, z_lo: 4; z = z_hi * 4 + z_lo), core: 2. Of those that a mesh axis runs over, the one named last changes fastest.
Arguments:
- amplitudes: bfloat16 [2, 2048, 2048], P(None, 'row', 'col'), may hold values from -6 to 6
- factor: bfloat16 [2048, 4096], P('row', 'col'), may hold values from -0.125 to 0.125
- kernel: float32 [4096, 4096], P('row', 'col'), may hold values from -6 to 6
Outputs:
- ladder: bfloat16 [2, 2048, 2048], P(None, 'row', 'col')
The draws below stay inside these ranges and needn't reach their ends.
All inputs are finite; a program needn't handle non-finite values.
Results may differ from the reference program's by a relative error of at most 0.015.
Values may be sent and summed in bfloat16 or wider, within the bound.
A program may use at most 64 MiB of HBM per device.

```python
import jax
import jax.numpy as jnp
from jax import lax

V = 2048
G = 4096
PAIRS = 2
GRID_COL = 256


def steps_of(key, shape, pieces, least, high):
    factor_of = 1.0
    for dim, blocks in pieces:
        steps = jax.random.uniform(jax.random.fold_in(jax.random.fold_in(key, 6), dim), (blocks,), jnp.float32, least / len(pieces), high / len(pieces))
        factor_of = factor_of * jnp.repeat(jnp.exp(steps), shape[dim] // blocks).reshape((-1,) + (1,) * (len(shape) - 1 - dim))
    return factor_of


def gaussian(key, dims, deviation, most, pieces=(), kind=jnp.bfloat16):
    entries = jax.random.normal(key, dims, jnp.float32) * deviation
    if len(pieces) > 0:
        entries = steps_of(key, dims, pieces, -0.22, 0.18) * entries
    return jnp.clip(entries, min=-most, max=most).astype(kind)


def setup_inputs(seed: int = 0) -> dict:
    splits = jax.random.split(jax.random.key(seed), 4)
    amplitudes = gaussian(splits[0], (PAIRS, V, V), 1.0, 6.0, ((1, 32), (2, 16)))
    factor = gaussian(splits[1], (V, G), V ** -0.5, 0.125, ((0, 32), (1, 16)))
    kernel = gaussian(splits[2], (G, G), 1.0, 6.0, ((0, 32), (1, 16)), jnp.float32)
    return {"amplitudes": amplitudes, "factor": factor, "kernel": kernel}


def reference(amplitudes, factor, kernel):
    block_count = G // GRID_COL

    def single_pair(amplitude_pair):
        projected = jnp.dot(amplitude_pair, factor, preferred_element_type=jnp.float32).astype(jnp.bfloat16)
        grid_pairs = jnp.dot(factor.T, projected, preferred_element_type=jnp.float32)
        scaled = (kernel * grid_pairs).astype(jnp.bfloat16)

        def add_block(running, block):
            start = (block * GRID_COL).astype(jnp.int32)
            scaled_part = lax.dynamic_slice_in_dim(scaled, start, GRID_COL, 1)
            factor_part = lax.dynamic_slice_in_dim(factor, start, GRID_COL, 1)
            term = jnp.dot(scaled_part, factor_part.T, preferred_element_type=jnp.float32).astype(jnp.bfloat16)
            term = lax.optimization_barrier(term)
            return running + term.astype(jnp.float32), None

        zeroed = jnp.zeros((G, V), jnp.float32)
        half_back, _ = lax.scan(add_block, zeroed, jnp.arange(block_count, dtype=jnp.int32))
        half_back = half_back.astype(jnp.bfloat16)
        return jnp.dot(factor, half_back, preferred_element_type=jnp.float32).astype(jnp.bfloat16)

    return lax.map(single_pair, amplitudes)
```

```python
import jax
import jax.numpy as jnp
from jax import lax
from jax.experimental import pallas as pl
from jax.experimental.pallas import tpu as pltpu
from jax.sharding import PartitionSpec as P

MESH = pl.DeviceIdType.MESH
F32, BF16 = jnp.float32, jnp.bfloat16
N = 4
DS = (1, 3, 2)


def dot(a, b, dims):
    return lax.dot_general(a, b, (dims, ((), ())), preferred_element_type=F32)


def kernel(
    a_ref, x_ref, k_ref, out_ref,
    kv, ag, xq, xp, tg, gacc, gr, wb, us, urx, us2, urz, osd, ory, os2, orz,
    lsem, s1, s2, s3, s4, s5, s6, s7, s8, s9, s10, sg, s11, s12, s13, s14,
):
    row, col = lax.axis_index("row"), lax.axis_index("col")
    k = lax.rem(row, 2)
    R = lax.div(row, 2)
    x, zl = lax.div(R, N), lax.rem(R, N)
    y, zh = lax.div(col, N), lax.rem(col, N)
    C = col

    def at(x=x, zl=zl, k=k, y=y, zh=zh):
        return ((x * N + zl) * 2 + k, y * N + zh)

    def plus(v, d):
        return lax.rem(v + d, N)

    mate = at(k=1 - k)
    flip = at(x=y, zl=zh, y=x, zh=zl)
    off_diagonal = R != C

    def remote(src, dst, sems, index, device):
        return pltpu.make_async_remote_copy(
            src_ref=src, dst_ref=dst, send_sem=sems.at[(0, *index)], recv_sem=sems.at[(1, *index)],
            device_id=device, device_id_type=MESH,
        )

    started = []

    def send(*args):
        copy = remote(*args)
        copy.start()
        started.append(copy)
        return copy

    own_a = pltpu.make_async_copy(a_ref, ag.at[C], lsem.at[0])
    own_x = pltpu.make_async_copy(x_ref, xq.at[R, k], lsem.at[1])
    own_k = pltpu.make_async_copy(k_ref, kv, lsem.at[2])
    own_p = pltpu.make_async_copy(x_ref, xp.at[R], lsem.at[3])
    for copy in (own_a, own_x, own_k):
        copy.start()

    barrier = pltpu.get_barrier_semaphore()
    partners = [mate]
    for d in DS:
        partners += [at(x=plus(x, d)), at(zl=plus(zl, d)), at(y=plus(y, d)), at(zh=plus(zh, d))]
    for device in partners:
        pl.semaphore_signal(barrier, inc=1, device_id=device, device_id_type=MESH)

    @pl.when(off_diagonal)
    def _():
        pl.semaphore_signal(barrier, inc=1, device_id=flip, device_id_type=MESH)
        pl.semaphore_wait(barrier, len(partners) + 1)

    @pl.when(jnp.logical_not(off_diagonal))
    def _():
        pl.semaphore_wait(barrier, len(partners))

    own_a.wait()
    own_x.wait()
    flipped = remote(x_ref, xp.at[R], s6, (0,), flip)
    a_z = {d: send(ag.at[C], ag.at[C], s1, (d,), at(zh=plus(zh, d))) for d in DS}
    x_z = {d: send(xq.at[R, k], xq.at[R, k], s3, (d,), at(zl=plus(zl, d))) for d in DS}

    def spread_a(dz):
        block = ag.at[y * N + plus(zh, N - dz)]
        return {d: send(block, block, s2, (dz, d), at(y=plus(y, d))) for d in DS}

    def spread_x(dz):
        block = xq.at[x * N + plus(zl, N - dz), k]
        return {d: send(block, block, s4, (dz, d), at(x=plus(x, d))) for d in DS}

    a_y, x_x = {}, {}
    a_y[0] = spread_a(0)
    x_x[0] = spread_x(0)

    @pl.when(off_diagonal)
    def _():
        flipped.start()

    @pl.when(jnp.logical_not(off_diagonal))
    def _():
        own_p.start()

    for dz in DS:
        x_z[dz].wait_recv()
        x_x[dz] = spread_x(dz)

    def share_x(dx):
        blocks = xq.at[pl.ds(plus(x, N - dx) * N, N), k]
        return send(blocks, blocks, s5, (dx,), mate)

    x_k = {0: share_x(0)}
    for dz in DS:
        a_z[dz].wait_recv()
        a_y[dz] = spread_a(dz)
    for dx in DS:
        for dz in (0, *DS):
            x_x[dz][dx].wait_recv()
        x_k[dx] = share_x(dx)

    for dx in (0, *DS):
        x_k[dx].wait_recv()
    acc = jnp.zeros((128, 256), F32)
    for dy in (0, *DS):
        ys = plus(y, N - dy)
        if dy:
            for dz in (0, *DS):
                a_y[dz][dy].wait_recv()
        for h in range(N):
            block = xq[ys * N + h].reshape(128, 256)
            acc += dot(ag[ys * N + h], block, ((1,), (0,)))
    tg[R, :, 0:256] = acc[0:64].astype(BF16)
    tg[R, :, 256:512] = acc[64:128].astype(BF16)

    t_z = {d: send(tg.at[R], tg.at[R], s9, (d,), at(zl=plus(zl, d))) for d in DS}

    def spread_t(dz):
        block = tg.at[x * N + plus(zl, N - dz)]
        return {d: send(block, block, s10, (dz, d), at(x=plus(x, d))) for d in DS}

    t_x = {0: spread_t(0)}

    @pl.when(off_diagonal)
    def _():
        flipped.wait_send()
        flipped.wait_recv()

    @pl.when(jnp.logical_not(off_diagonal))
    def _():
        own_p.wait()

    p_z = {d: send(xp.at[C], xp.at[C], s7, (d,), at(zh=plus(zh, d))) for d in DS}

    def spread_p(dz):
        block = xp.at[y * N + plus(zh, N - dz)]
        return {d: send(block, block, s8, (dz, d), at(y=plus(y, d))) for d in DS}

    p_y = {0: spread_p(0)}
    for dz in DS:
        t_z[dz].wait_recv()
        t_x[dz] = spread_t(dz)
    for dz in DS:
        p_z[dz].wait_recv()
        p_y[dz] = spread_p(dz)
    for dz in (0, *DS):
        for dy in DS:
            p_y[dz][dy].wait_recv()

    acc = jnp.zeros((256, 512), F32)
    for dx in (0, *DS):
        xs = plus(x, N - dx) * N
        if dx:
            for dz in (0, *DS):
                t_x[dz][dx].wait_recv()
        left = xp[pl.ds(xs, N)].reshape(256, 256)
        right = tg[pl.ds(xs, N)].reshape(256, 512)
        acc += dot(left, right, ((0,), (0,)))
    gacc[...] = acc
    mine, theirs = pl.ds(k * 128, 128), pl.ds((1 - k) * 128, 128)
    send(gacc.at[theirs], gr, sg, (0,), mate).wait_recv()
    own_k.wait()
    kern = kv[...]
    for p in range(2):
        half = slice(p * 256, p * 256 + 256)
        wb[mine, half] = (kern * (gacc[mine, half] + gr[:, half])).astype(BF16)
    send(wb.at[mine], wb.at[mine], sg, (1,), mate).wait_recv()

    w = wb[...]
    u_x = {}
    for dx in (*DS, 0):
        xs = plus(x, dx) * N
        part = dot(xp[pl.ds(xs, N)].reshape(256, 256), w, ((1,), (0,)))
        if dx:
            us[dx] = part.reshape(N, 64, 512).astype(BF16)
            u_x[dx] = send(us.at[dx], urx.at[dx], s11, (dx,), at(x=plus(x, dx)))
    us2[...] = part.reshape(N, 64, 512)
    for dx in DS:
        u_x[dx].wait_recv()
        us2[...] += urx[dx].astype(F32)
    u_z = {}
    for d in DS:
        us[0, d] = us2[plus(zl, d)].astype(BF16)
        u_z[d] = send(us.at[0, d], urz.at[d], s12, (d,), at(zl=plus(zl, d)))
    total = us2[zl]
    for d in DS:
        u_z[d].wait_recv()
        total += urz[d].astype(F32)
    total = total.astype(BF16)
    left = jnp.concatenate([total[:, 0:256], total[:, 256:512]], axis=0)

    o_y = {}
    for dy in (*DS, 0):
        ys = plus(y, dy) * N
        for h in range(N):
            part = dot(left, xq[ys + h].reshape(128, 256), ((1,), (1,)))
            if dy:
                osd[dy, h] = part.astype(BF16)
            else:
                os2[h] = part
        if dy:
            o_y[dy] = send(osd.at[dy], ory.at[dy], s13, (dy,), at(y=plus(y, dy)))
    for dy in DS:
        o_y[dy].wait_recv()
        os2[...] += ory[dy].astype(F32)
    o_z = {}
    for d in DS:
        osd[0, d] = os2[plus(zh, d)].astype(BF16)
        o_z[d] = send(osd.at[0, d], orz.at[d], s14, (d,), at(zh=plus(zh, d)))
    total = os2[zh]
    for d in DS:
        o_z[d].wait_recv()
        total += orz[d].astype(F32)
    out_ref[...] = total.astype(BF16)
    for copy in started:
        copy.wait_send()


def per_device(amplitudes, factor, kern):
    any_spec = pl.BlockSpec(memory_space=pl.ANY)
    vmem = pltpu.VMEM
    dma = pltpu.SemaphoreType.DMA
    result = pl.pallas_call(
        kernel,
        name="ladder",
        out_shape=jax.ShapeDtypeStruct((128, 128), BF16),
        in_specs=[any_spec] * 3,
        out_specs=pl.BlockSpec(memory_space=vmem),
        scratch_shapes=[
            vmem((128, 256), F32),
            vmem((16, 128, 128), BF16),
            vmem((16, 2, 64, 256), BF16),
            vmem((16, 64, 256), BF16),
            vmem((16, 64, 512), BF16),
            vmem((256, 512), F32),
            vmem((128, 512), F32),
            vmem((256, 512), BF16),
            vmem((4, 4, 64, 512), BF16),
            vmem((4, 4, 64, 512), BF16),
            vmem((4, 64, 512), F32),
            vmem((4, 64, 512), BF16),
            vmem((4, 4, 128, 128), BF16),
            vmem((4, 4, 128, 128), BF16),
            vmem((4, 128, 128), F32),
            vmem((4, 128, 128), BF16),
            dma((4,)),
            dma((2, 4)), dma((2, 4, 4)), dma((2, 4)), dma((2, 4, 4)), dma((2, 4)), dma((2, 1)),
            dma((2, 4)), dma((2, 4, 4)), dma((2, 4)), dma((2, 4, 4)), dma((2, 2)), dma((2, 4)),
            dma((2, 4)), dma((2, 4)), dma((2, 4)),
        ],
        compiler_params=pltpu.CompilerParams(collective_id=0, has_side_effects=True),
    )(amplitudes.reshape(128, 128), factor, kern)
    return result.reshape(2, 64, 128)


def solution(mesh):
    placed = (P(None, "row", "col"), P("row", "col"), P("row", "col"))
    return jax.shard_map(
        per_device, mesh=mesh, in_specs=placed, out_specs=P(None, "row", "col"), check_vma=False
    )
```

```python
import jax
import jax.numpy as jnp
from jax import lax
from jax.experimental import pallas as pl
from jax.experimental.pallas import tpu as pltpu
from jax.sharding import PartitionSpec as P

MESH = pl.DeviceIdType.MESH
F32, BF16 = jnp.float32, jnp.bfloat16
N = 4
DS = (1, 3, 2)
COPIES = 240


def dot(a, b, dims):
    return lax.dot_general(a, b, (dims, ((), ())), preferred_element_type=F32)


def kernel(
    a_ref, x_ref, k_ref, out_ref,
    kv, ag, xq, xf, xp, tg, gacc, gr, wb, us, urx, us2, urz, osd, ory, os2, orz, lsem, sems,
):
    row, col = lax.axis_index("row"), lax.axis_index("col")
    k = lax.rem(row, 2)
    R = lax.div(row, 2)
    x, zl = lax.div(R, N), lax.rem(R, N)
    y, zh = lax.div(col, N), lax.rem(col, N)
    C = col

    def at(x=x, zl=zl, k=k, y=y, zh=zh):
        return ((x * N + zl) * 2 + k, y * N + zh)

    def plus(v, d):
        return lax.rem(v + d, N)

    def minus(v, d):
        return lax.rem(v + N - d, N)

    mate = at(k=1 - k)
    flip = at(x=y, y=x)
    up, down = at(zh=plus(zh, 1)), at(zh=plus(zh, 3))
    swaps = x != y
    root = zl == zh

    used = [0]
    started = []

    def remote(src, dst, device):
        index = used[0]
        used[0] += 1
        return pltpu.make_async_remote_copy(
            src_ref=src, dst_ref=dst, send_sem=sems.at[0, index], recv_sem=sems.at[1, index],
            device_id=device, device_id_type=MESH,
        )

    def send(src, dst, device):
        copy = remote(src, dst, device)
        copy.start()
        started.append(copy)
        return copy

    def otherwise(condition):
        return pl.when(jnp.logical_not(condition))

    own_a = pltpu.make_async_copy(a_ref, ag.at[:, C], lsem.at[0])
    own_x = pltpu.make_async_copy(x_ref, xq.at[R, k], lsem.at[1])
    own_k = pltpu.make_async_copy(k_ref, kv, lsem.at[2])
    own_f = pltpu.make_async_copy(x_ref, xf, lsem.at[3])
    own_p = pltpu.make_async_copy(xf, xp.at[y * N + zl], lsem.at[4])
    for copy in (own_a, own_x, own_k):
        copy.start()

    barrier = pltpu.get_barrier_semaphore()
    partners = [up, down, mate]
    for d in DS:
        partners += [at(x=plus(x, d)), at(zl=plus(zl, d)), at(y=plus(y, d))]
    for device in partners:
        pl.semaphore_signal(barrier, inc=1, device_id=device, device_id_type=MESH)

    @pl.when(swaps)
    def _():
        pl.semaphore_signal(barrier, inc=1, device_id=flip, device_id_type=MESH)
        pl.semaphore_wait(barrier, len(partners) + 1)

    @otherwise(swaps)
    def _():
        own_f.start()
        pl.semaphore_wait(barrier, len(partners))

    own_a.wait()
    own_x.wait()

    def a_block(p, dz):
        return ag.at[p, y * N + minus(zh, dz)]

    a_z, a_y, x_x = {}, {}, {}

    def spread_a(p, dz):
        block = a_block(p, dz)
        for d in DS:
            a_y[p, dz, d] = send(block, block, at(y=plus(y, d)))

    def spread_x(dz):
        block = xq.at[x * N + minus(zl, dz), k]
        for d in DS:
            x_x[dz, d] = send(block, block, at(x=plus(x, d)))

    def pass_a(p, dz, ahead):
        block = a_block(p, dz)
        return send(block, block, up if ahead else down)

    a_up, a_down, a_far = {}, {}, {}
    a_up[0], a_down[0] = pass_a(0, 0, True), pass_a(0, 0, False)
    x_z = {d: send(xq.at[R, k], xq.at[R, k], at(zl=plus(zl, d))) for d in DS}
    a_down[1], a_up[1] = pass_a(1, 0, False), pass_a(1, 0, True)
    spread_a(0, 0)
    spread_x(0)
    flipped = remote(x_ref, xf, flip)

    @pl.when(swaps)
    def _():
        flipped.start()

    spread_a(1, 0)
    for dz in DS:
        x_z[dz].wait_recv()
        spread_x(dz)

    a_up[0].wait_recv()
    a_far[0] = pass_a(0, 1, True)
    spread_a(0, 1)
    a_down[0].wait_recv()
    spread_a(0, 3)
    a_down[1].wait_recv()
    a_far[1] = pass_a(1, 3, False)
    a_up[1].wait_recv()

    @pl.when(swaps)
    def _():
        flipped.wait_send()
        flipped.wait_recv()

    @otherwise(swaps)
    def _():
        own_f.wait()

    mine_p = [pl.ds(y * N, 2), pl.ds(y * N + 2, 2)]
    collect = {d: remote(xf, xp.at[y * N + zl], at(zl=zh)) for d in DS}

    for d in DS:
        @pl.when(minus(zl, zh) == d)
        def _():
            collect[d].start()

    @pl.when(root)
    def _():
        own_p.start()

    spread_a(1, 3)
    spread_a(1, 1)

    def share_x(dx):
        blocks = xq.at[pl.ds(minus(x, dx) * N, N), k]
        return send(blocks, blocks, mate)

    x_k = {0: share_x(0)}
    for dx in DS:
        for dz in (0, *DS):
            x_x[dz, dx].wait_recv()
        x_k[dx] = share_x(dx)

    a_far[0].wait_recv()
    spread_a(0, 2)
    a_far[1].wait_recv()
    spread_a(1, 2)

    low = [remote(xp.at[s], xp.at[s], up) for s in mine_p]
    high = [remote(xp.at[s], xp.at[s], down) for s in mine_p]
    turn = minus(zh, zl)

    @pl.when(root)
    def _():
        own_p.wait()
        for d in DS:
            collect[d].wait_recv()
        low[0].start()
        high[1].start()
        low[1].start()
        high[0].start()

    def project(p):
        acc = jnp.zeros((64, 256), F32)
        for dy in (0, *DS):
            ys = minus(y, dy) * N
            if dy:
                for dz in (0, *DS):
                    a_y[p, dz, dy].wait_recv()
            left = jnp.concatenate([ag[p, ys + h] for h in range(N)], axis=1)
            acc += dot(left, xq[pl.ds(ys, N)].reshape(512, 256), ((1,), (0,)))
        tg[p, R] = acc.astype(BF16)

    def spread_t(p, dz):
        block = tg.at[p, x * N + minus(zl, dz)]
        for d in DS:
            t_x[p, dz, d] = send(block, block, at(x=plus(x, d)))

    t_z, t_x = {}, {}
    for dx in (0, *DS):
        x_k[dx].wait_recv()
    for p in range(2):
        project(p)
        for d in DS:
            t_z[p, d] = send(tg.at[p, R], tg.at[p, R], at(zl=plus(zl, d)))
        if p == 0:
            spread_t(0, 0)
    for dz in DS:
        t_z[0, dz].wait_recv()
        spread_t(0, dz)
    spread_t(1, 0)

    @pl.when(turn == 1)
    def _():
        low[0].wait_recv()
        low[0].start()
        low[1].wait_recv()

    @pl.when(turn == 3)
    def _():
        high[1].wait_recv()
        high[1].start()
        high[0].wait_recv()

    for dz in DS:
        t_z[1, dz].wait_recv()
        spread_t(1, dz)

    @pl.when(turn == 2)
    def _():
        low[0].wait_recv()
        high[1].wait_recv()

    line = xp.at[pl.ds(y * N, N)]
    p_y = [send(line, line, at(y=plus(y, d))) for d in DS]
    for copy in p_y:
        copy.wait_recv()

    mine, theirs = pl.ds(k * 128, 128), pl.ds((1 - k) * 128, 128)
    u_x, u_z, o_y, o_z = {}, {}, {}, {}

    def middle(p):
        acc = jnp.zeros((256, 256), F32)
        for dx in (0, *DS):
            xs = minus(x, dx) * N
            if dx:
                for dz in (0, *DS):
                    t_x[p, dz, dx].wait_recv()
            left = xp[pl.ds(xs, N)].reshape(256, 256)
            right = tg[p, pl.ds(xs, N)].reshape(256, 256)
            acc += dot(left, right, ((0,), (0,)))
        gacc[p] = acc
        send(gacc.at[p, theirs], gr.at[p], mate).wait_recv()
        wb[p, mine] = (kv[...] * (gacc[p, mine] + gr[p])).astype(BF16)
        send(wb.at[p, mine], wb.at[p, mine], mate).wait_recv()
        w = wb[p]
        for dx in (*DS, 0):
            xs = plus(x, dx) * N
            part = dot(xp[pl.ds(xs, N)].reshape(256, 256), w, ((1,), (0,))).reshape(N, 64, 256)
            if dx:
                us[p, dx] = part.astype(BF16)
            else:
                us2[p] = part
        for e in (*DS, 0):
            for dx in DS:
                place = us.at[p, dx, plus(zl, e)]
                u_x[p, dx, e] = send(place, urx.at[p, dx, e], at(x=plus(x, dx)))

    def sum_x(p):
        for e in (*DS, 0):
            part = us2[p, plus(zl, e)]
            for dx in DS:
                u_x[p, dx, e].wait_recv()
                part += urx[p, dx, e].astype(F32)
            if e:
                us[p, 0, e] = part.astype(BF16)
                u_z[p, e] = send(us.at[p, 0, e], urz.at[p, e], at(zl=plus(zl, e)))
            else:
                us2[p, zl] = part

    def sum_z(p):
        part = us2[p, zl]
        for e in DS:
            u_z[p, e].wait_recv()
            part += urz[p, e].astype(F32)
        u = part.astype(BF16)
        for dy in (*DS, 0):
            ys = plus(y, dy) * N
            part = dot(u, xq[pl.ds(ys, N)].reshape(512, 256), ((1,), (1,)))
            for h in range(N):
                piece = part[:, h * 128 : h * 128 + 128]
                if dy:
                    osd[p, dy, h] = piece.astype(BF16)
                else:
                    os2[p, h] = piece
        for e in (2, 1, 3, 0):
            for dy in DS:
                place = osd.at[p, dy, plus(zh, e)]
                o_y[p, dy, e] = send(place, ory.at[p, dy, e], at(y=plus(y, dy)))

    def sum_y(p):
        for e in (2, 1, 3, 0):
            part = os2[p, plus(zh, e)]
            for dy in DS:
                o_y[p, dy, e].wait_recv()
                part += ory[p, dy, e].astype(F32)
            if e == 2 or e == (3 if p == 0 else 1):
                osd[p, 0, e] = part.astype(BF16)
                ahead = p == 0 if e == 2 else e == 1
                o_z[p, e] = send(osd.at[p, 0, e], orz.at[p, e], up if ahead else down)
            else:
                os2[p, plus(zh, e)] = part

    def pass_o(p):
        e = 1 if p == 0 else 3
        o_z[p, 2].wait_recv()
        osd[p, 0, e] = (os2[p, plus(zh, e)] + orz[p, 2].astype(F32)).astype(BF16)
        o_z[p, e] = send(osd.at[p, 0, e], orz.at[p, e], up if e == 1 else down)

    def finish(p):
        part = os2[p, zh]
        for e in ((3, 1) if p == 0 else (1, 3)):
            o_z[p, e].wait_recv()
            part += orz[p, e].astype(F32)
        out_ref[p] = part.astype(BF16)

    own_k.wait()
    middle(0)
    middle(1)
    sum_x(0)
    sum_z(0)
    sum_x(1)
    sum_y(0)
    sum_z(1)
    pass_o(0)
    sum_y(1)
    pass_o(1)
    finish(0)
    finish(1)

    for copy in started:
        copy.wait_send()
    for d in DS:
        @pl.when(minus(zl, zh) == d)
        def _():
            collect[d].wait_send()

    @pl.when(root)
    def _():
        for copy in (*low, *high):
            copy.wait_send()

    @pl.when(turn == 1)
    def _():
        low[0].wait_send()

    @pl.when(turn == 3)
    def _():
        high[1].wait_send()


def per_device(amplitudes, factor, kern):
    any_spec = pl.BlockSpec(memory_space=pl.ANY)
    vmem = pltpu.VMEM
    dma = pltpu.SemaphoreType.DMA
    return pl.pallas_call(
        kernel,
        name="ladder",
        out_shape=jax.ShapeDtypeStruct((2, 64, 128), BF16),
        in_specs=[any_spec] * 3,
        out_specs=pl.BlockSpec(memory_space=vmem),
        scratch_shapes=[
            vmem((128, 256), F32),
            vmem((2, 16, 64, 128), BF16),
            vmem((16, 2, 64, 256), BF16),
            vmem((64, 256), BF16),
            vmem((16, 64, 256), BF16),
            vmem((2, 16, 64, 256), BF16),
            vmem((2, 256, 256), F32),
            vmem((2, 128, 256), F32),
            vmem((2, 256, 256), BF16),
            vmem((2, 4, 4, 64, 256), BF16),
            vmem((2, 4, 4, 64, 256), BF16),
            vmem((2, 4, 64, 256), F32),
            vmem((2, 4, 64, 256), BF16),
            vmem((2, 4, 4, 64, 128), BF16),
            vmem((2, 4, 4, 64, 128), BF16),
            vmem((2, 4, 64, 128), F32),
            vmem((2, 4, 64, 128), BF16),
            dma((5,)),
            dma((2, COPIES)),
        ],
        compiler_params=pltpu.CompilerParams(collective_id=0, has_side_effects=True),
    )(amplitudes, factor, kern)


def solution(mesh):
    placed = (P(None, "row", "col"), P("row", "col"), P("row", "col"))
    return jax.shard_map(
        per_device, mesh=mesh, in_specs=placed, out_specs=P(None, "row", "col"), check_vma=False
    )
```

```python
import math

import jax
import jax.numpy as jnp
from jax import lax
from jax.experimental import pallas as pl
from jax.experimental.pallas import tpu as pltpu
from jax.sharding import PartitionSpec as P

MESH = pl.DeviceIdType.MESH
F32, BF16 = jnp.float32, jnp.bfloat16
N = 4
DS = (1, 3, 2)
COPIES = 66
UNIT = 64 * 128
UNITS = 290


def dot(a, b, dims):
    return lax.dot_general(a, b, (dims, ((), ())), preferred_element_type=F32)


def kernel(
    a_ref, x_ref, k_ref, out_ref,
    kv, ag, xq, xf, xp, tg, gacc, gr, wb, us, urx, us2, urz, osd, ory, os2, orz, all_sent, lsem, ssem, rsem,
):
    row, col = lax.axis_index("row"), lax.axis_index("col")
    k = lax.rem(row, 2)
    R = lax.div(row, 2)
    x, zl = lax.div(R, N), lax.rem(R, N)
    y, zh = lax.div(col, N), lax.rem(col, N)
    C = col

    def at(x=x, zl=zl, k=k, y=y, zh=zh):
        return ((x * N + zl) * 2 + k, y * N + zh)

    def plus(v, d):
        return lax.rem(v + d, N)

    def minus(v, d):
        return lax.rem(v + N - d, N)

    mate = at(k=1 - k)
    flip = at(x=y, y=x)
    up, down = at(zh=plus(zh, 1)), at(zh=plus(zh, 3))
    swaps = x != y
    root = zl == zh

    used = [0]
    sent = [0]

    def group():
        used[0] += 1
        return used[0] - 1

    def remote(src, dst, device, number, mine=0):
        return pltpu.make_async_remote_copy(
            src_ref=src, dst_ref=dst, send_sem=ssem.at[mine], recv_sem=rsem.at[number],
            device_id=device, device_id_type=MESH,
        )

    def send(src, dst, device, number):
        remote(src, dst, device, number).start()
        sent[0] += math.prod(src.shape) * src.dtype.itemsize // 2 // UNIT

    def arrived(ref, number):
        remote(ref, ref, mate, number).wait_recv()

    def otherwise(condition):
        return pl.when(jnp.logical_not(condition))

    own_a = pltpu.make_async_copy(a_ref, ag.at[:, C], lsem.at[0])
    own_x = pltpu.make_async_copy(x_ref, xq.at[R, k], lsem.at[1])
    own_k = pltpu.make_async_copy(k_ref, kv, lsem.at[2])
    own_f = pltpu.make_async_copy(x_ref, xf, lsem.at[3])
    own_p = pltpu.make_async_copy(xf, xp.at[y * N + zl], lsem.at[4])
    for copy in (own_a, own_x, own_k):
        copy.start()

    barrier = pltpu.get_barrier_semaphore()
    partners = [up, down, mate]
    for d in DS:
        partners += [at(x=plus(x, d)), at(zl=plus(zl, d)), at(y=plus(y, d))]
    for device in partners:
        pl.semaphore_signal(barrier, inc=1, device_id=device, device_id_type=MESH)

    @pl.when(swaps)
    def _():
        pl.semaphore_signal(barrier, inc=1, device_id=flip, device_id_type=MESH)
        pl.semaphore_wait(barrier, len(partners) + 1)

    @otherwise(swaps)
    def _():
        own_f.start()
        pl.semaphore_wait(barrier, len(partners))

    own_a.wait()
    own_x.wait()

    def a_block(p, dz):
        return ag.at[p, y * N + minus(zh, dz)]

    def x_block(dz):
        return xq.at[x * N + minus(zl, dz), k]

    def t_block(p, dz):
        return tg.at[p, x * N + minus(zl, dz)]

    a_ring = {(p, dz): group() for p in range(2) for dz in DS}
    a_y = {(p, d): group() for p in range(2) for d in DS}
    x_z, x_x, x_k = {d: group() for d in DS}, {d: group() for d in DS}, group()
    t_z = {(p, d): group() for p in range(2) for d in DS}
    t_x = {(p, d): group() for p in range(2) for d in DS}
    f_x, f_z, f_y = group(), group(), group()

    def ring_a(p, dz, device, number):
        send(a_block(p, dz), a_block(p, dz), device, a_ring[p, number])

    def spread_a(p, dz):
        for d in DS:
            send(a_block(p, dz), a_block(p, dz), at(y=plus(y, d)), a_y[p, d])

    def spread_x(dz):
        for d in DS:
            send(x_block(dz), x_block(dz), at(x=plus(x, d)), x_x[d])

    def spread_t(p, dz):
        for d in DS:
            send(t_block(p, dz), t_block(p, dz), at(x=plus(x, d)), t_x[p, d])

    def share_x(dx):
        blocks = xq.at[pl.ds(minus(x, dx) * N, N), k]
        send(blocks, blocks, mate, x_k)

    ring_a(0, 0, up, 1)
    ring_a(0, 0, down, 3)
    for d in DS:
        send(x_block(0), x_block(0), at(zl=plus(zl, d)), x_z[d])
    flipped = remote(x_ref, xf, flip, f_x, 1)

    @pl.when(swaps)
    def _():
        flipped.start()

    spread_x(0)
    spread_a(0, 0)
    spread_a(1, 0)
    for dz in DS:
        arrived(x_block(dz), x_z[dz])
        spread_x(dz)
    ring_a(1, 0, down, 3)
    ring_a(1, 0, up, 1)
    arrived(a_block(0, 1), a_ring[0, 1])
    ring_a(0, 1, up, 2)
    spread_a(0, 1)

    @pl.when(swaps)
    def _():
        flipped.wait_send()
        flipped.wait_recv()

    @otherwise(swaps)
    def _():
        own_f.wait()

    collect = remote(xf, xp.at[y * N + zl], at(zl=zh), f_z, 2)

    @pl.when(root)
    def _():
        own_p.start()

    @otherwise(root)
    def _():
        collect.start()

    arrived(a_block(0, 3), a_ring[0, 3])
    spread_a(0, 3)
    share_x(0)

    halves = [xp.at[pl.ds(y * N, 2)], xp.at[pl.ds(y * N + 2, 2)]]
    low = [remote(s, s, up, group(), 3 + i) for i, s in enumerate(halves)]
    high = [remote(s, s, down, group(), 5 + i) for i, s in enumerate(halves)]
    turn = minus(zh, zl)

    @pl.when(root)
    def _():
        own_p.wait()
        arrived(xp.at[pl.ds(0, 3)], f_z)
        low[0].start()
        high[1].start()
        low[1].start()
        high[0].start()

    for dx in DS:
        arrived(xq.at[pl.ds(minus(x, dx) * N, N), k], x_x[dx])
        share_x(dx)
    arrived(a_block(0, 2), a_ring[0, 2])
    spread_a(0, 2)
    arrived(a_block(1, 3), a_ring[1, 3])
    ring_a(1, 3, down, 2)
    spread_a(1, 3)
    arrived(a_block(1, 1), a_ring[1, 1])
    spread_a(1, 1)

    def project(p):
        acc = jnp.zeros((64, 256), F32)
        for dy in (0, *DS):
            ys = minus(y, dy) * N
            if dy:
                arrived(ag.at[p, pl.ds(ys, N)], a_y[p, dy])
            left = jnp.concatenate([ag[p, ys + h] for h in range(N)], axis=1)
            acc += dot(left, xq[pl.ds(ys, N)].reshape(512, 256), ((1,), (0,)))
        tg[p, R] = acc.astype(BF16)
        for d in DS:
            send(t_block(p, 0), t_block(p, 0), at(zl=plus(zl, d)), t_z[p, d])

    arrived(xq.at[:, 1 - k], x_k)
    project(0)
    spread_t(0, 0)

    @pl.when(turn == 1)
    def _():
        low[0].wait_recv()
        low[0].start()
        low[1].wait_recv()

    @pl.when(turn == 3)
    def _():
        high[1].wait_recv()
        high[1].start()
        high[0].wait_recv()

    arrived(a_block(1, 2), a_ring[1, 2])
    spread_a(1, 2)
    for dz in DS:
        arrived(t_block(0, dz), t_z[0, dz])
        spread_t(0, dz)
    project(1)

    @pl.when(turn == 2)
    def _():
        low[0].wait_recv()
        high[1].wait_recv()

    line = xp.at[pl.ds(y * N, N)]
    for d in DS:
        send(line, line, at(y=plus(y, d)), f_y)
    spread_t(1, 0)
    for dz in DS:
        arrived(t_block(1, dz), t_z[1, dz])
        spread_t(1, dz)
    arrived(xp.at[pl.ds(0, 12)], f_y)

    mine, theirs = pl.ds(k * 128, 128), pl.ds((1 - k) * 128, 128)
    back = (*DS, 0)
    to_mate = {(p, i): group() for p in range(2) for i in range(2)}
    u_x = {(p, e): group() for p in range(2) for e in back}
    u_z = {p: group() for p in range(2)}
    o_y = {(p, e): group() for p in range(2) for e in back}
    o_z = {(p, e): group() for p in range(2) for e in DS}

    def middle(p):
        acc = jnp.zeros((256, 256), F32)
        for dx in (0, *DS):
            xs = minus(x, dx) * N
            if dx:
                arrived(tg.at[p, pl.ds(xs, N)], t_x[p, dx])
            left = xp[pl.ds(xs, N)].reshape(256, 256)
            right = tg[p, pl.ds(xs, N)].reshape(256, 256)
            acc += dot(left, right, ((0,), (0,)))
        gacc[p] = acc
        send(gacc.at[p, theirs], gr.at[p], mate, to_mate[p, 0])
        arrived(gr.at[p], to_mate[p, 0])
        wb[p, mine] = (kv[...] * (gacc[p, mine] + gr[p])).astype(BF16)
        send(wb.at[p, mine], wb.at[p, mine], mate, to_mate[p, 1])
        arrived(wb.at[p, theirs], to_mate[p, 1])
        w = wb[p]
        for dx in (*DS, 0):
            xs = plus(x, dx) * N
            part = dot(xp[pl.ds(xs, N)].reshape(256, 256), w, ((1,), (0,))).reshape(N, 64, 256)
            if dx:
                us[p, dx] = part.astype(BF16)
            else:
                us2[p] = part
        for e in (*DS, 0):
            for dx in DS:
                place = us.at[p, dx, plus(zl, e)]
                send(place, urx.at[p, e, dx], at(x=plus(x, dx)), u_x[p, e])

    def sum_x(p):
        for e in (*DS, 0):
            part = us2[p, plus(zl, e)]
            arrived(urx.at[p, e, pl.ds(1, 3)], u_x[p, e])
            for dx in DS:
                part += urx[p, e, dx].astype(F32)
            if e:
                us[p, 0, e] = part.astype(BF16)
                send(us.at[p, 0, e], urz.at[p, e], at(zl=plus(zl, e)), u_z[p])
            else:
                us2[p, zl] = part

    def sum_z(p):
        part = us2[p, zl]
        arrived(urz.at[p, pl.ds(1, 3)], u_z[p])
        for e in DS:
            part += urz[p, e].astype(F32)
        u = part.astype(BF16)
        for dy in (*DS, 0):
            ys = plus(y, dy) * N
            part = dot(u, xq[pl.ds(ys, N)].reshape(512, 256), ((1,), (1,)))
            for h in range(N):
                piece = part[:, h * 128 : h * 128 + 128]
                if dy:
                    osd[p, dy, h] = piece.astype(BF16)
                else:
                    os2[p, h] = piece
        for e in (2, 1, 3, 0):
            for dy in DS:
                place = osd.at[p, dy, plus(zh, e)]
                send(place, ory.at[p, e, dy], at(y=plus(y, dy)), o_y[p, e])

    def sum_y(p):
        for e in (2, 1, 3, 0):
            part = os2[p, plus(zh, e)]
            arrived(ory.at[p, e, pl.ds(1, 3)], o_y[p, e])
            for dy in DS:
                part += ory[p, e, dy].astype(F32)
            if e == 2 or e == (3 if p == 0 else 1):
                osd[p, 0, e] = part.astype(BF16)
                ahead = p == 0 if e == 2 else e == 1
                send(osd.at[p, 0, e], orz.at[p, e], up if ahead else down, o_z[p, e])
            else:
                os2[p, plus(zh, e)] = part

    def pass_o(p):
        e = 1 if p == 0 else 3
        arrived(orz.at[p, 2], o_z[p, 2])
        osd[p, 0, e] = (os2[p, plus(zh, e)] + orz[p, 2].astype(F32)).astype(BF16)
        send(osd.at[p, 0, e], orz.at[p, e], up if e == 1 else down, o_z[p, e])

    def finish(p):
        part = os2[p, zh]
        for e in ((3, 1) if p == 0 else (1, 3)):
            arrived(orz.at[p, e], o_z[p, e])
            part += orz[p, e].astype(F32)
        out_ref[p] = part.astype(BF16)

    own_k.wait()
    middle(0)
    middle(1)
    sum_x(0)
    sum_x(1)
    sum_z(0)
    sum_z(1)
    sum_y(0)
    pass_o(0)
    sum_y(1)
    pass_o(1)
    finish(0)
    finish(1)

    assert sent[0] == UNITS and used[0] <= COPIES, (sent[0], used[0])
    remote(all_sent, all_sent, mate, 0).wait_send()

    @otherwise(root)
    def _():
        collect.wait_send()

    @pl.when(root)
    def _():
        for copy in (*low, *high):
            copy.wait_send()

    @pl.when(turn == 1)
    def _():
        low[0].wait_send()

    @pl.when(turn == 3)
    def _():
        high[1].wait_send()


def per_device(amplitudes, factor, kern):
    any_spec = pl.BlockSpec(memory_space=pl.ANY)
    vmem = pltpu.VMEM
    dma = pltpu.SemaphoreType.DMA
    return pl.pallas_call(
        kernel,
        name="ladder",
        out_shape=jax.ShapeDtypeStruct((2, 64, 128), BF16),
        in_specs=[any_spec] * 3,
        out_specs=pl.BlockSpec(memory_space=vmem),
        scratch_shapes=[
            vmem((128, 256), F32),
            vmem((2, 16, 64, 128), BF16),
            vmem((16, 2, 64, 256), BF16),
            vmem((64, 256), BF16),
            vmem((16, 64, 256), BF16),
            vmem((2, 16, 64, 256), BF16),
            vmem((2, 256, 256), F32),
            vmem((2, 128, 256), F32),
            vmem((2, 256, 256), BF16),
            vmem((2, 4, 4, 64, 256), BF16),
            vmem((2, 4, 4, 64, 256), BF16),
            vmem((2, 4, 64, 256), F32),
            vmem((2, 4, 64, 256), BF16),
            vmem((2, 4, 4, 64, 128), BF16),
            vmem((2, 4, 4, 64, 128), BF16),
            vmem((2, 4, 64, 128), F32),
            vmem((2, 4, 64, 128), BF16),
            vmem((UNITS, 64, 128), BF16),
            dma((5,)),
            dma((7,)),
            dma((COPIES,)),
        ],
        compiler_params=pltpu.CompilerParams(collective_id=0, has_side_effects=True),
    )(amplitudes, factor, kern)


def solution(mesh):
    placed = (P(None, "row", "col"), P("row", "col"), P("row", "col"))
    return jax.shard_map(
        per_device, mesh=mesh, in_specs=placed, out_specs=P(None, "row", "col"), check_vma=False
    )
```

```python
import math

import jax
import jax.numpy as jnp
from jax import lax
from jax.experimental import pallas as pl
from jax.experimental.pallas import tpu as pltpu
from jax.sharding import PartitionSpec as P

MESH = pl.DeviceIdType.MESH
F32, BF16 = jnp.float32, jnp.bfloat16
N = 4
DS = (1, 3, 2)
COPIES = 86
UNIT = 64 * 128
UNITS = 290


def dot(a, b, dims):
    return lax.dot_general(a, b, (dims, ((), ())), preferred_element_type=F32)


def kernel(
    a_ref, x_ref, k_ref, out_ref,
    kv, ag, xq, xf, xp, tg, gacc, gr, wb, us, urx, us2, urz, osd, ory, os2, orz, all_sent, lsem, ssem, rsem,
):
    row, col = lax.axis_index("row"), lax.axis_index("col")
    k = lax.rem(row, 2)
    R = lax.div(row, 2)
    x, zl = lax.div(R, N), lax.rem(R, N)
    y, zh = lax.div(col, N), lax.rem(col, N)
    C = col

    def at(x=x, zl=zl, k=k, y=y, zh=zh):
        return ((x * N + zl) * 2 + k, y * N + zh)

    def plus(v, d):
        return lax.rem(v + d, N)

    def minus(v, d):
        return lax.rem(v + N - d, N)

    mate = at(k=1 - k)
    flip = at(x=y, y=x)
    up, down = at(zh=plus(zh, 1)), at(zh=plus(zh, 3))
    swaps = x != y
    root = zl == zh

    used = [0]
    sent = [0]

    def group():
        used[0] += 1
        return used[0] - 1

    def remote(src, dst, device, number, mine=0):
        return pltpu.make_async_remote_copy(
            src_ref=src, dst_ref=dst, send_sem=ssem.at[mine], recv_sem=rsem.at[number],
            device_id=device, device_id_type=MESH,
        )

    def send(src, dst, device, number):
        remote(src, dst, device, number).start()
        sent[0] += math.prod(src.shape) * src.dtype.itemsize // 2 // UNIT

    def arrived(ref, number):
        remote(ref, ref, mate, number).wait_recv()

    def otherwise(condition):
        return pl.when(jnp.logical_not(condition))

    own_a = pltpu.make_async_copy(a_ref, ag.at[:, C], lsem.at[0])
    own_x = pltpu.make_async_copy(x_ref, xq.at[R, k], lsem.at[1])
    own_k = pltpu.make_async_copy(k_ref, kv, lsem.at[2])
    own_f = pltpu.make_async_copy(x_ref, xf, lsem.at[3])
    own_p = pltpu.make_async_copy(xf, xp.at[y * N + zl], lsem.at[4])
    for copy in (own_a, own_x, own_k):
        copy.start()

    barrier = pltpu.get_barrier_semaphore()
    partners = [up, down, mate]
    for d in DS:
        partners += [at(x=plus(x, d)), at(zl=plus(zl, d)), at(y=plus(y, d))]
    for device in partners:
        pl.semaphore_signal(barrier, inc=1, device_id=device, device_id_type=MESH)

    @pl.when(swaps)
    def _():
        pl.semaphore_signal(barrier, inc=1, device_id=flip, device_id_type=MESH)
        pl.semaphore_wait(barrier, len(partners) + 1)

    @otherwise(swaps)
    def _():
        own_f.start()
        pl.semaphore_wait(barrier, len(partners))

    own_a.wait()
    own_x.wait()

    def a_block(p, dz):
        return ag.at[p, y * N + minus(zh, dz)]

    def x_block(dz):
        return xq.at[x * N + minus(zl, dz), k]

    def t_block(p, dz, dx=0):
        return tg.at[p, minus(x, dx) * N + minus(zl, dz)]

    a_ring = {(p, dz): group() for p in range(2) for dz in DS}
    a_y = {(p, d): group() for p in range(2) for d in DS}
    x_z, x_x, x_k = {d: group() for d in DS}, {d: group() for d in DS}, group()
    t_z = {(p, d): group() for p in range(2) for d in DS}
    t_x = {(p, d, dz): group() for p in range(2) for d in (1, 3) for dz in range(N)}
    t_far = {p: group() for p in range(2)}
    f_x, f_z, f_y = group(), group(), group()

    def ring_a(p, dz, device, number):
        send(a_block(p, dz), a_block(p, dz), device, a_ring[p, number])

    def spread_a(p, dz):
        for d in DS:
            send(a_block(p, dz), a_block(p, dz), at(y=plus(y, d)), a_y[p, d])

    def spread_x(dz):
        for d in DS:
            send(x_block(dz), x_block(dz), at(x=plus(x, d)), x_x[d])

    def spread_t(p, dz):
        for d in (1, 3):
            send(t_block(p, dz), t_block(p, dz), at(x=plus(x, d)), t_x[p, d, dz])

    def relay_t(p):
        for dz, d in ((0, 1), (1, 3), (3, 1), (2, 3)):
            block = t_block(p, dz, d)
            arrived(block, t_x[p, d, dz])
            send(block, block, at(x=plus(x, d)), t_far[p])

    def share_x(dx):
        blocks = xq.at[pl.ds(minus(x, dx) * N, N), k]
        send(blocks, blocks, mate, x_k)

    ring_a(0, 0, up, 1)
    ring_a(0, 0, down, 3)
    for d in DS:
        send(x_block(0), x_block(0), at(zl=plus(zl, d)), x_z[d])
    flipped = remote(x_ref, xf, flip, f_x, 1)

    @pl.when(swaps)
    def _():
        flipped.start()

    spread_x(0)
    spread_a(0, 0)
    spread_a(1, 0)
    for dz in DS:
        arrived(x_block(dz), x_z[dz])
        spread_x(dz)
    ring_a(1, 0, down, 3)
    ring_a(1, 0, up, 1)
    arrived(a_block(0, 1), a_ring[0, 1])
    ring_a(0, 1, up, 2)
    spread_a(0, 1)

    @pl.when(swaps)
    def _():
        flipped.wait_send()
        flipped.wait_recv()

    @otherwise(swaps)
    def _():
        own_f.wait()

    collect = remote(xf, xp.at[y * N + zl], at(zl=zh), f_z, 2)

    @pl.when(root)
    def _():
        own_p.start()

    @otherwise(root)
    def _():
        collect.start()

    arrived(a_block(0, 3), a_ring[0, 3])
    spread_a(0, 3)
    share_x(0)

    halves = [xp.at[pl.ds(y * N, 2)], xp.at[pl.ds(y * N + 2, 2)]]
    low = [remote(s, s, up, group(), 3 + i) for i, s in enumerate(halves)]
    high = [remote(s, s, down, group(), 5 + i) for i, s in enumerate(halves)]
    turn = minus(zh, zl)

    @pl.when(root)
    def _():
        own_p.wait()
        arrived(xp.at[pl.ds(0, 3)], f_z)
        low[0].start()
        high[1].start()
        low[1].start()
        high[0].start()

    for dx in DS:
        arrived(xq.at[pl.ds(minus(x, dx) * N, N), k], x_x[dx])
        share_x(dx)
    arrived(a_block(0, 2), a_ring[0, 2])
    spread_a(0, 2)
    arrived(a_block(1, 3), a_ring[1, 3])
    ring_a(1, 3, down, 2)
    spread_a(1, 3)
    arrived(a_block(1, 1), a_ring[1, 1])
    spread_a(1, 1)

    def project(p):
        acc = jnp.zeros((64, 256), F32)
        for dy in (0, *DS):
            ys = minus(y, dy) * N
            if dy:
                arrived(ag.at[p, pl.ds(ys, N)], a_y[p, dy])
            left = jnp.concatenate([ag[p, ys + h] for h in range(N)], axis=1)
            acc += dot(left, xq[pl.ds(ys, N)].reshape(512, 256), ((1,), (0,)))
        tg[p, R] = acc.astype(BF16)
        for d in DS:
            send(t_block(p, 0), t_block(p, 0), at(zl=plus(zl, d)), t_z[p, d])

    arrived(xq.at[:, 1 - k], x_k)
    project(0)
    spread_t(0, 0)

    @pl.when(turn == 1)
    def _():
        low[0].wait_recv()
        low[0].start()

    @pl.when(turn == 3)
    def _():
        high[1].wait_recv()
        high[1].start()

    arrived(a_block(1, 2), a_ring[1, 2])
    spread_a(1, 2)
    for dz in DS:
        arrived(t_block(0, dz), t_z[0, dz])
        spread_t(0, dz)
    project(1)

    relay_t(0)

    @pl.when(turn == 1)
    def _():
        low[1].wait_recv()

    @pl.when(turn == 3)
    def _():
        high[0].wait_recv()

    @pl.when(turn == 2)
    def _():
        low[0].wait_recv()
        high[1].wait_recv()

    line = xp.at[pl.ds(y * N, N)]
    for d in DS:
        send(line, line, at(y=plus(y, d)), f_y)
    spread_t(1, 0)
    for dz in DS:
        arrived(t_block(1, dz), t_z[1, dz])
        spread_t(1, dz)
    relay_t(1)
    arrived(xp.at[pl.ds(0, 12)], f_y)

    mine, theirs = pl.ds(k * 128, 128), pl.ds((1 - k) * 128, 128)
    back = (*DS, 0)
    to_mate = {(p, i): group() for p in range(2) for i in range(2)}
    u_x = {(p, e): group() for p in range(2) for e in back}
    u_far = {(p, e): group() for p in range(2) for e in back}
    u_z = {p: group() for p in range(2)}
    o_y = {(p, e): group() for p in range(2) for e in back}
    o_z = {(p, e): group() for p in range(2) for e in DS}

    via = {0: 1, 3: 1, 1: 3, 2: 3}

    def middle(p):
        acc = jnp.zeros((256, 256), F32)
        for dx in (0, *DS):
            xs = minus(x, dx) * N
            if dx:
                for dz, d in ((0, 3), (1, 1), (3, 3), (2, 1)):
                    if d == dx:
                        arrived(t_block(p, dz, d), t_x[p, d, dz])
                if dx == 2:
                    arrived(tg.at[p, pl.ds(xs, N)], t_far[p])
            left = xp[pl.ds(xs, N)].reshape(256, 256)
            right = tg[p, pl.ds(xs, N)].reshape(256, 256)
            acc += dot(left, right, ((0,), (0,)))
        gacc[p] = acc
        send(gacc.at[p, theirs], gr.at[p], mate, to_mate[p, 0])
        arrived(gr.at[p], to_mate[p, 0])
        wb[p, mine] = (kv[...] * (gacc[p, mine] + gr[p])).astype(BF16)
        send(wb.at[p, mine], wb.at[p, mine], mate, to_mate[p, 1])
        arrived(wb.at[p, theirs], to_mate[p, 1])
        w = wb[p]
        for dx in (*DS, 0):
            xs = plus(x, dx) * N
            part = dot(xp[pl.ds(xs, N)].reshape(256, 256), w, ((1,), (0,))).reshape(N, 64, 256)
            if dx:
                us[p, dx] = part.astype(BF16)
            else:
                us2[p] = part
        for e in back:
            send(us.at[p, 2, plus(zl, e)], urx.at[p, e, 2], at(x=plus(x, via[e])), u_far[p, e])
        for e in back:
            d = 4 - via[e]
            send(us.at[p, d, plus(zl, e)], urx.at[p, e, d], at(x=plus(x, d)), u_x[p, e])

    def relay_u(p):
        for e in back:
            d, h = via[e], plus(zl, e)
            arrived(urx.at[p, e, 2], u_far[p, e])
            us[p, d, h] = (us[p, d, h].astype(F32) + urx[p, e, 2].astype(F32)).astype(BF16)
            send(us.at[p, d, h], urx.at[p, e, d], at(x=plus(x, d)), u_x[p, e])

    def sum_x(p):
        for e in (*DS, 0):
            part = us2[p, plus(zl, e)]
            arrived(urx.at[p, e, pl.ds(0, 2)], u_x[p, e])
            for dx in (1, 3):
                part += urx[p, e, dx].astype(F32)
            if e:
                us[p, 0, e] = part.astype(BF16)
                send(us.at[p, 0, e], urz.at[p, e], at(zl=plus(zl, e)), u_z[p])
            else:
                us2[p, zl] = part

    def sum_z(p):
        part = us2[p, zl]
        arrived(urz.at[p, pl.ds(1, 3)], u_z[p])
        for e in DS:
            part += urz[p, e].astype(F32)
        u = part.astype(BF16)
        for dy in (*DS, 0):
            ys = plus(y, dy) * N
            part = dot(u, xq[pl.ds(ys, N)].reshape(512, 256), ((1,), (1,)))
            for h in range(N):
                piece = part[:, h * 128 : h * 128 + 128]
                if dy:
                    osd[p, dy, h] = piece.astype(BF16)
                else:
                    os2[p, h] = piece
        for e in (2, 1, 3, 0):
            for dy in DS:
                place = osd.at[p, dy, plus(zh, e)]
                send(place, ory.at[p, e, dy], at(y=plus(y, dy)), o_y[p, e])

    def sum_y(p):
        for e in (2, 1, 3, 0):
            part = os2[p, plus(zh, e)]
            arrived(ory.at[p, e, pl.ds(1, 3)], o_y[p, e])
            for dy in DS:
                part += ory[p, e, dy].astype(F32)
            if e == 2 or e == (3 if p == 0 else 1):
                osd[p, 0, e] = part.astype(BF16)
                ahead = p == 0 if e == 2 else e == 1
                send(osd.at[p, 0, e], orz.at[p, e], up if ahead else down, o_z[p, e])
            else:
                os2[p, plus(zh, e)] = part

    def pass_o(p):
        e = 1 if p == 0 else 3
        arrived(orz.at[p, 2], o_z[p, 2])
        osd[p, 0, e] = (os2[p, plus(zh, e)] + orz[p, 2].astype(F32)).astype(BF16)
        send(osd.at[p, 0, e], orz.at[p, e], up if e == 1 else down, o_z[p, e])

    def finish(p):
        part = os2[p, zh]
        for e in ((3, 1) if p == 0 else (1, 3)):
            arrived(orz.at[p, e], o_z[p, e])
            part += orz[p, e].astype(F32)
        out_ref[p] = part.astype(BF16)

    own_k.wait()
    middle(0)
    middle(1)
    relay_u(0)
    relay_u(1)
    sum_x(0)
    sum_x(1)
    sum_z(0)
    sum_z(1)
    sum_y(0)
    sum_y(1)
    pass_o(0)
    pass_o(1)
    finish(0)
    finish(1)

    assert sent[0] == UNITS and used[0] <= COPIES, (sent[0], used[0])
    remote(all_sent, all_sent, mate, 0).wait_send()

    @otherwise(root)
    def _():
        collect.wait_send()

    @pl.when(root)
    def _():
        for copy in (*low, *high):
            copy.wait_send()

    @pl.when(turn == 1)
    def _():
        low[0].wait_send()

    @pl.when(turn == 3)
    def _():
        high[1].wait_send()


def per_device(amplitudes, factor, kern):
    any_spec = pl.BlockSpec(memory_space=pl.ANY)
    vmem = pltpu.VMEM
    dma = pltpu.SemaphoreType.DMA
    return pl.pallas_call(
        kernel,
        name="ladder",
        out_shape=jax.ShapeDtypeStruct((2, 64, 128), BF16),
        in_specs=[any_spec] * 3,
        out_specs=pl.BlockSpec(memory_space=vmem),
        scratch_shapes=[
            vmem((128, 256), F32),
            vmem((2, 16, 64, 128), BF16),
            vmem((16, 2, 64, 256), BF16),
            vmem((64, 256), BF16),
            vmem((16, 64, 256), BF16),
            vmem((2, 16, 64, 256), BF16),
            vmem((2, 256, 256), F32),
            vmem((2, 128, 256), F32),
            vmem((2, 256, 256), BF16),
            vmem((2, 4, 4, 64, 256), BF16),
            vmem((2, 4, 4, 64, 256), BF16),
            vmem((2, 4, 64, 256), F32),
            vmem((2, 4, 64, 256), BF16),
            vmem((2, 4, 4, 64, 128), BF16),
            vmem((2, 4, 4, 64, 128), BF16),
            vmem((2, 4, 64, 128), F32),
            vmem((2, 4, 64, 128), BF16),
            vmem((UNITS, 64, 128), BF16),
            dma((5,)),
            dma((7,)),
            dma((COPIES,)),
        ],
        compiler_params=pltpu.CompilerParams(collective_id=0, has_side_effects=True),
    )(amplitudes, factor, kern)


def solution(mesh):
    placed = (P(None, "row", "col"), P("row", "col"), P("row", "col"))
    return jax.shard_map(
        per_device, mesh=mesh, in_specs=placed, out_specs=P(None, "row", "col"), check_vma=False
    )
```

```python
import math

import jax
import jax.numpy as jnp
from jax import lax
from jax.experimental import pallas as pl
from jax.experimental.pallas import tpu as pltpu
from jax.sharding import PartitionSpec as P

MESH = pl.DeviceIdType.MESH
F32, BF16 = jnp.float32, jnp.bfloat16
N = 4
DS = (1, 3, 2)
COPIES = 88
UNIT = 64 * 128
UNITS = 294


def dot(a, b, dims):
    return lax.dot_general(a, b, (dims, ((), ())), preferred_element_type=F32)


def kernel(
    a_ref, x_ref, k_ref, out_ref,
    kv, ag, xq, xf, xp, tg, gacc, gr, wb, us, urx, us2, urz, osd, ory, os2, orz, all_sent, lsem, ssem, rsem,
):
    row, col = lax.axis_index("row"), lax.axis_index("col")
    k = lax.rem(row, 2)
    R = lax.div(row, 2)
    x, zl = lax.div(R, N), lax.rem(R, N)
    y, zh = lax.div(col, N), lax.rem(col, N)
    C = col

    def at(x=x, zl=zl, k=k, y=y, zh=zh):
        return ((x * N + zl) * 2 + k, y * N + zh)

    def plus(v, d):
        return lax.rem(v + d, N)

    def minus(v, d):
        return lax.rem(v + N - d, N)

    mate = at(k=1 - k)
    flip = at(x=y, y=x)
    up, down = at(zh=plus(zh, 1)), at(zh=plus(zh, 3))
    swaps = x != y
    root = zl == zh

    used = [0]
    sent = [0]

    def group():
        used[0] += 1
        return used[0] - 1

    def remote(src, dst, device, number, mine=0):
        return pltpu.make_async_remote_copy(
            src_ref=src, dst_ref=dst, send_sem=ssem.at[mine], recv_sem=rsem.at[number],
            device_id=device, device_id_type=MESH,
        )

    def send(src, dst, device, number):
        remote(src, dst, device, number).start()
        sent[0] += math.prod(src.shape) * src.dtype.itemsize // 2 // UNIT

    def arrived(ref, number):
        remote(ref, ref, mate, number).wait_recv()

    def otherwise(condition):
        return pl.when(jnp.logical_not(condition))

    own_a = pltpu.make_async_copy(a_ref, ag.at[:, C], lsem.at[0])
    own_x = pltpu.make_async_copy(x_ref, xq.at[R, k], lsem.at[1])
    own_k = pltpu.make_async_copy(k_ref, kv, lsem.at[2])
    own_f = pltpu.make_async_copy(x_ref, xf, lsem.at[3])
    own_p = pltpu.make_async_copy(xf, xp.at[y * N + zl], lsem.at[4])
    for copy in (own_a, own_x, own_k):
        copy.start()

    barrier = pltpu.get_barrier_semaphore()
    partners = [up, down, mate]
    for d in DS:
        partners += [at(x=plus(x, d)), at(zl=plus(zl, d)), at(y=plus(y, d))]
    for device in partners:
        pl.semaphore_signal(barrier, inc=1, device_id=device, device_id_type=MESH)

    @pl.when(swaps)
    def _():
        pl.semaphore_signal(barrier, inc=1, device_id=flip, device_id_type=MESH)
        pl.semaphore_wait(barrier, len(partners) + 1)

    @otherwise(swaps)
    def _():
        own_f.start()
        pl.semaphore_wait(barrier, len(partners))

    own_a.wait()
    own_x.wait()

    def a_block(p, dz):
        return ag.at[p, y * N + minus(zh, dz)]

    def x_block(dz):
        return xq.at[x * N + minus(zl, dz), k]

    def t_block(p, dz, dx=0):
        return tg.at[p, minus(x, dx) * N + minus(zl, dz)]

    a_ring = {(p, dz): group() for p in range(2) for dz in DS}
    a_y = {(p, d): group() for p in range(2) for d in DS}
    x_z, x_x, x_k = {d: group() for d in DS}, {d: group() for d in DS}, group()
    t_z = {(p, d): group() for p in range(2) for d in DS}
    t_x = {(p, d, dz): group() for p in range(2) for d in (1, 3) for dz in range(N)}
    t_far = {p: group() for p in range(2)}
    f_x, f_z, f_y = group(), group(), group()

    def ring_a(p, dz, device, number):
        send(a_block(p, dz), a_block(p, dz), device, a_ring[p, number])

    def spread_a(p, dz):
        for d in DS:
            send(a_block(p, dz), a_block(p, dz), at(y=plus(y, d)), a_y[p, d])

    def spread_x(dz):
        for d in DS:
            send(x_block(dz), x_block(dz), at(x=plus(x, d)), x_x[d])

    def spread_t(p, dz):
        for d in (1, 3):
            send(t_block(p, dz), t_block(p, dz), at(x=plus(x, d)), t_x[p, d, dz])

    def relay_t(p):
        for dz, d in ((0, 1), (1, 3), (3, 1), (2, 3)):
            block = t_block(p, dz, d)
            arrived(block, t_x[p, d, dz])
            send(block, block, at(x=plus(x, d)), t_far[p])

    def share_x(dx):
        blocks = xq.at[pl.ds(minus(x, dx) * N, N), k]
        send(blocks, blocks, mate, x_k)

    ring_a(0, 0, up, 1)
    ring_a(1, 0, down, 3)
    for d in DS:
        send(x_block(0), x_block(0), at(zl=plus(zl, d)), x_z[d])
    ring_a(0, 0, down, 3)
    ring_a(1, 0, up, 1)
    flipped = remote(x_ref, xf, flip, f_x, 1)

    @pl.when(swaps)
    def _():
        flipped.start()

    spread_x(0)
    spread_a(0, 0)
    spread_a(1, 0)
    arrived(x_block(1), x_z[1])
    spread_x(1)
    arrived(x_block(3), x_z[3])
    spread_x(3)

    @pl.when(swaps)
    def _():
        flipped.wait_send()
        flipped.wait_recv()

    @otherwise(swaps)
    def _():
        own_f.wait()

    place = xp.at[y * N + zl]
    collect = remote(xf, place, at(zl=zh), f_z, 2)
    from_below, from_above = [group(), group()], [group(), group()]
    half = lax.div(zl, 2)
    halves = [xp.at[pl.ds(y * N, 2)], xp.at[pl.ds(y * N + 2, 2)]]
    onward_up, onward_down = remote(halves[0], halves[0], up, group(), 3), remote(halves[1], halves[1], down, group(), 4)
    turn = minus(zh, zl)

    @pl.when(root)
    def _():
        own_p.start()

    @otherwise(root)
    def _():
        collect.start()

    arrived(x_block(2), x_z[2])
    spread_x(2)
    arrived(a_block(0, 1), a_ring[0, 1])
    ring_a(0, 1, up, 2)
    spread_a(0, 1)
    arrived(a_block(1, 3), a_ring[1, 3])
    ring_a(1, 3, down, 2)
    send(xf, place, at(zl=zh, zh=plus(zh, 1)), from_below[0] + half)
    send(xf, place, at(zl=zh, zh=plus(zh, 3)), from_above[0] + half)
    spread_a(1, 3)
    arrived(a_block(0, 3), a_ring[0, 3])
    spread_a(0, 3)
    arrived(a_block(1, 1), a_ring[1, 1])
    spread_a(1, 1)
    share_x(0)

    for dx in DS:
        arrived(xq.at[pl.ds(minus(x, dx) * N, N), k], x_x[dx])
        share_x(dx)
    arrived(a_block(0, 2), a_ring[0, 2])
    spread_a(0, 2)
    arrived(a_block(1, 2), a_ring[1, 2])
    spread_a(1, 2)

    def project(p):
        acc = jnp.zeros((64, 256), F32)
        for dy in (0, *DS):
            ys = minus(y, dy) * N
            if dy:
                arrived(ag.at[p, pl.ds(ys, N)], a_y[p, dy])
            left = jnp.concatenate([ag[p, ys + h] for h in range(N)], axis=1)
            acc += dot(left, xq[pl.ds(ys, N)].reshape(512, 256), ((1,), (0,)))
        tg[p, R] = acc.astype(BF16)
        for d in DS:
            send(t_block(p, 0), t_block(p, 0), at(zl=plus(zl, d)), t_z[p, d])

    arrived(xq.at[:, 1 - k], x_k)
    @pl.when(turn == 1)
    def _():
        arrived(halves[0], from_below[0])
        onward_up.start()

    @pl.when(turn == 3)
    def _():
        arrived(halves[1], from_above[1])
        onward_down.start()

    project(0)
    spread_t(0, 0)

    project(1)
    spread_t(1, 0)
    for dz in DS:
        arrived(t_block(0, dz), t_z[0, dz])
        spread_t(0, dz)

    @pl.when(root)
    def _():
        own_p.wait()
        arrived(xp.at[pl.ds(0, 3)], f_z)

    @pl.when(turn == 1)
    def _():
        arrived(halves[1], from_below[1])

    @pl.when(turn == 3)
    def _():
        arrived(halves[0], from_above[0])

    @pl.when(turn == 2)
    def _():
        onward_up.wait_recv()
        onward_down.wait_recv()

    line = xp.at[pl.ds(y * N, N)]
    for d in DS:
        send(line, line, at(y=plus(y, d)), f_y)
    for dz in DS:
        arrived(t_block(1, dz), t_z[1, dz])
        spread_t(1, dz)
    relay_t(0)
    relay_t(1)
    arrived(xp.at[pl.ds(0, 12)], f_y)

    mine, theirs = pl.ds(k * 128, 128), pl.ds((1 - k) * 128, 128)
    back = (*DS, 0)
    to_mate = {(p, i): group() for p in range(2) for i in range(2)}
    u_x = {(p, e): group() for p in range(2) for e in back}
    u_far = {(p, e): group() for p in range(2) for e in back}
    u_z = {p: group() for p in range(2)}
    o_y = {(p, e): group() for p in range(2) for e in back}
    o_z = {(p, e): group() for p in range(2) for e in DS}

    via = {0: 1, 3: 1, 1: 3, 2: 3}

    def pairs_part(p):
        acc = jnp.zeros((256, 256), F32)
        for dx in (0, *DS):
            xs = minus(x, dx) * N
            if dx:
                for dz, d in ((0, 3), (1, 1), (3, 3), (2, 1)):
                    if d == dx:
                        arrived(t_block(p, dz, d), t_x[p, d, dz])
                if dx == 2:
                    arrived(tg.at[p, pl.ds(xs, N)], t_far[p])
            left = xp[pl.ds(xs, N)].reshape(256, 256)
            right = tg[p, pl.ds(xs, N)].reshape(256, 256)
            acc += dot(left, right, ((0,), (0,)))
        gacc[p] = acc
        send(gacc.at[p, theirs], gr.at[p], mate, to_mate[p, 0])

    def scale(p):
        arrived(gr.at[p], to_mate[p, 0])
        wb[p, mine] = (kv[...] * (gacc[p, mine] + gr[p])).astype(BF16)
        send(wb.at[p, mine], wb.at[p, mine], mate, to_mate[p, 1])

    def first_back(p):
        arrived(wb.at[p, theirs], to_mate[p, 1])
        w = wb[p]
        for dx in (*DS, 0):
            xs = plus(x, dx) * N
            part = dot(xp[pl.ds(xs, N)].reshape(256, 256), w, ((1,), (0,))).reshape(N, 64, 256)
            if dx:
                us[p, dx] = part.astype(BF16)
            else:
                us2[p] = part
        for e in back:
            send(us.at[p, 2, plus(zl, e)], urx.at[p, e, 2], at(x=plus(x, via[e])), u_far[p, e])
        for e in back:
            d = 4 - via[e]
            send(us.at[p, d, plus(zl, e)], urx.at[p, e, d], at(x=plus(x, d)), u_x[p, e])

    def relay_u(p):
        for e in back:
            d, h = via[e], plus(zl, e)
            arrived(urx.at[p, e, 2], u_far[p, e])
            us[p, d, h] = (us[p, d, h].astype(F32) + urx[p, e, 2].astype(F32)).astype(BF16)
            send(us.at[p, d, h], urx.at[p, e, d], at(x=plus(x, d)), u_x[p, e])

    def sum_x(p):
        for e in (*DS, 0):
            part = us2[p, plus(zl, e)]
            arrived(urx.at[p, e, pl.ds(0, 2)], u_x[p, e])
            for dx in (1, 3):
                part += urx[p, e, dx].astype(F32)
            if e:
                us[p, 0, e] = part.astype(BF16)
                send(us.at[p, 0, e], urz.at[p, e], at(zl=plus(zl, e)), u_z[p])
            else:
                us2[p, zl] = part

    def sum_z(p):
        part = us2[p, zl]
        arrived(urz.at[p, pl.ds(1, 3)], u_z[p])
        for e in DS:
            part += urz[p, e].astype(F32)
        u = part.astype(BF16)
        for dy in (*DS, 0):
            ys = plus(y, dy) * N
            part = dot(u, xq[pl.ds(ys, N)].reshape(512, 256), ((1,), (1,)))
            for h in range(N):
                piece = part[:, h * 128 : h * 128 + 128]
                if dy:
                    osd[p, dy, h] = piece.astype(BF16)
                else:
                    os2[p, h] = piece
        for e in (2, 1, 3, 0):
            for dy in DS:
                place = osd.at[p, dy, plus(zh, e)]
                send(place, ory.at[p, e, dy], at(y=plus(y, dy)), o_y[p, e])

    def sum_y(p):
        for e in (2, 1, 3, 0):
            part = os2[p, plus(zh, e)]
            arrived(ory.at[p, e, pl.ds(1, 3)], o_y[p, e])
            for dy in DS:
                part += ory[p, e, dy].astype(F32)
            if e == 2 or e == (3 if p == 0 else 1):
                osd[p, 0, e] = part.astype(BF16)
                ahead = p == 0 if e == 2 else e == 1
                send(osd.at[p, 0, e], orz.at[p, e], up if ahead else down, o_z[p, e])
            else:
                os2[p, plus(zh, e)] = part

    def pass_o(p):
        e = 1 if p == 0 else 3
        arrived(orz.at[p, 2], o_z[p, 2])
        osd[p, 0, e] = (os2[p, plus(zh, e)] + orz[p, 2].astype(F32)).astype(BF16)
        send(osd.at[p, 0, e], orz.at[p, e], up if e == 1 else down, o_z[p, e])

    def finish(p):
        part = os2[p, zh]
        for e in ((3, 1) if p == 0 else (1, 3)):
            arrived(orz.at[p, e], o_z[p, e])
            part += orz[p, e].astype(F32)
        out_ref[p] = part.astype(BF16)

    own_k.wait()
    pairs_part(0)
    pairs_part(1)
    scale(0)
    scale(1)
    first_back(0)
    first_back(1)
    relay_u(0)
    relay_u(1)
    sum_x(0)
    sum_x(1)
    sum_z(0)
    sum_z(1)
    sum_y(0)
    sum_y(1)
    pass_o(0)
    pass_o(1)
    finish(0)
    finish(1)

    assert sent[0] == UNITS and used[0] <= COPIES, (sent[0], used[0])
    remote(all_sent, all_sent, mate, 0).wait_send()

    @otherwise(root)
    def _():
        collect.wait_send()

    @pl.when(turn == 1)
    def _():
        onward_up.wait_send()

    @pl.when(turn == 3)
    def _():
        onward_down.wait_send()


def per_device(amplitudes, factor, kern):
    any_spec = pl.BlockSpec(memory_space=pl.ANY)
    vmem = pltpu.VMEM
    dma = pltpu.SemaphoreType.DMA
    return pl.pallas_call(
        kernel,
        name="ladder",
        out_shape=jax.ShapeDtypeStruct((2, 64, 128), BF16),
        in_specs=[any_spec] * 3,
        out_specs=pl.BlockSpec(memory_space=vmem),
        scratch_shapes=[
            vmem((128, 256), F32),
            vmem((2, 16, 64, 128), BF16),
            vmem((16, 2, 64, 256), BF16),
            vmem((64, 256), BF16),
            vmem((16, 64, 256), BF16),
            vmem((2, 16, 64, 256), BF16),
            vmem((2, 256, 256), F32),
            vmem((2, 128, 256), F32),
            vmem((2, 256, 256), BF16),
            vmem((2, 4, 4, 64, 256), BF16),
            vmem((2, 4, 4, 64, 256), BF16),
            vmem((2, 4, 64, 256), F32),
            vmem((2, 4, 64, 256), BF16),
            vmem((2, 4, 4, 64, 128), BF16),
            vmem((2, 4, 4, 64, 128), BF16),
            vmem((2, 4, 64, 128), F32),
            vmem((2, 4, 64, 128), BF16),
            vmem((UNITS, 64, 128), BF16),
            dma((5,)),
            dma((5,)),
            dma((COPIES,)),
        ],
        compiler_params=pltpu.CompilerParams(collective_id=0, has_side_effects=True),
    )(amplitudes, factor, kern)


def solution(mesh):
    placed = (P(None, "row", "col"), P("row", "col"), P("row", "col"))
    return jax.shard_map(
        per_device, mesh=mesh, in_specs=placed, out_specs=P(None, "row", "col"), check_vma=False
    )
```

```python
import math

import jax
import jax.numpy as jnp
from jax import lax
from jax.experimental import pallas as pl
from jax.experimental.pallas import tpu as pltpu
from jax.sharding import PartitionSpec as P

MESH = pl.DeviceIdType.MESH
F32, BF16 = jnp.float32, jnp.bfloat16
N = 4
DS = (1, 3, 2)
COPIES = 87
UNIT = 64 * 128
UNITS = 310


def dot(a, b, dims):
    return lax.dot_general(a, b, (dims, ((), ())), preferred_element_type=F32)


def kernel(
    a_ref, x_ref, k_ref, out_ref,
    kv, ag, xq, xf, xp, tg, gacc, gr, us, urx, us2, urz, osd, ory, os2, orz, all_sent, lsem, ssem, rsem,
):
    row, col = lax.axis_index("row"), lax.axis_index("col")
    k = lax.rem(row, 2)
    R = lax.div(row, 2)
    x, zl = lax.div(R, N), lax.rem(R, N)
    y, zh = lax.div(col, N), lax.rem(col, N)
    C = col

    def at(x=x, zl=zl, k=k, y=y, zh=zh):
        return ((x * N + zl) * 2 + k, y * N + zh)

    def plus(v, d):
        return lax.rem(v + d, N)

    def minus(v, d):
        return lax.rem(v + N - d, N)

    mate = at(k=1 - k)
    flip = at(x=y, y=x)
    up, down = at(zh=plus(zh, 1)), at(zh=plus(zh, 3))
    swaps = x != y
    root = zl == zh

    used = [0]
    sent = [0]

    def group():
        used[0] += 1
        return used[0] - 1

    def remote(src, dst, device, number, mine=0):
        return pltpu.make_async_remote_copy(
            src_ref=src, dst_ref=dst, send_sem=ssem.at[mine], recv_sem=rsem.at[number],
            device_id=device, device_id_type=MESH,
        )

    def send(src, dst, device, number):
        remote(src, dst, device, number).start()
        sent[0] += math.prod(src.shape) * src.dtype.itemsize // 2 // UNIT

    def arrived(ref, number):
        remote(ref, ref, mate, number).wait_recv()

    def otherwise(condition):
        return pl.when(jnp.logical_not(condition))

    own_a = pltpu.make_async_copy(a_ref, ag.at[:, C], lsem.at[0])
    own_x = pltpu.make_async_copy(x_ref, xq.at[R, k], lsem.at[1])
    mine, theirs = pl.ds(k * 128, 128), pl.ds((1 - k) * 128, 128)
    own_k = pltpu.make_async_copy(k_ref, kv.at[mine], lsem.at[2])
    own_f = pltpu.make_async_copy(x_ref, xf, lsem.at[3])
    own_p = pltpu.make_async_copy(xf, xp.at[y * N + zl], lsem.at[4])
    for copy in (own_a, own_x, own_k):
        copy.start()

    barrier = pltpu.get_barrier_semaphore()
    partners = [up, down, mate]
    for d in DS:
        partners += [at(x=plus(x, d)), at(zl=plus(zl, d)), at(y=plus(y, d))]
    for device in partners:
        pl.semaphore_signal(barrier, inc=1, device_id=device, device_id_type=MESH)

    @pl.when(swaps)
    def _():
        pl.semaphore_signal(barrier, inc=1, device_id=flip, device_id_type=MESH)
        pl.semaphore_wait(barrier, len(partners) + 1)

    @otherwise(swaps)
    def _():
        own_f.start()
        pl.semaphore_wait(barrier, len(partners))

    own_a.wait()
    own_x.wait()
    own_k.wait()
    mate_k = group()

    def a_block(p, dz):
        return ag.at[p, y * N + minus(zh, dz)]

    def x_block(dz):
        return xq.at[x * N + minus(zl, dz), k]

    def t_block(p, dz, dx=0):
        return tg.at[p, minus(x, dx) * N + minus(zl, dz)]

    a_ring = {(p, dz): group() for p in range(2) for dz in DS}
    a_y = {(p, d): group() for p in range(2) for d in DS}
    x_z, x_x, x_k = {d: group() for d in DS}, {d: group() for d in DS}, group()
    t_z = {(p, d): group() for p in range(2) for d in DS}
    t_x = {(p, d, dz): group() for p in range(2) for d in (1, 3) for dz in range(N)}
    t_far = {p: group() for p in range(2)}
    f_x, f_z, f_y = group(), group(), group()

    def ring_a(p, dz, device, number):
        send(a_block(p, dz), a_block(p, dz), device, a_ring[p, number])

    def spread_a(p, dz):
        for d in DS:
            send(a_block(p, dz), a_block(p, dz), at(y=plus(y, d)), a_y[p, d])

    def spread_x(dz):
        for d in DS:
            send(x_block(dz), x_block(dz), at(x=plus(x, d)), x_x[d])

    def spread_t(p, dz):
        for d in (1, 3):
            send(t_block(p, dz), t_block(p, dz), at(x=plus(x, d)), t_x[p, d, dz])

    def relay_t(p):
        for dz, d in ((0, 1), (1, 3), (3, 1), (2, 3)):
            block = t_block(p, dz, d)
            arrived(block, t_x[p, d, dz])
            send(block, block, at(x=plus(x, d)), t_far[p])

    def share_x(dx):
        blocks = xq.at[pl.ds(minus(x, dx) * N, N), k]
        send(blocks, blocks, mate, x_k)

    ring_a(0, 0, up, 1)
    ring_a(1, 0, down, 3)
    for d in DS:
        send(x_block(0), x_block(0), at(zl=plus(zl, d)), x_z[d])
    ring_a(0, 0, down, 3)
    ring_a(1, 0, up, 1)
    flipped = remote(x_ref, xf, flip, f_x, 1)

    @pl.when(swaps)
    def _():
        flipped.start()

    spread_x(0)
    spread_a(0, 0)
    spread_a(1, 0)
    arrived(x_block(1), x_z[1])
    spread_x(1)
    arrived(x_block(3), x_z[3])
    spread_x(3)

    @pl.when(swaps)
    def _():
        flipped.wait_send()
        flipped.wait_recv()

    @otherwise(swaps)
    def _():
        own_f.wait()

    place = xp.at[y * N + zl]
    collect = remote(xf, place, at(zl=zh), f_z, 2)
    from_below, from_above = [group(), group()], [group(), group()]
    half = lax.div(zl, 2)
    halves = [xp.at[pl.ds(y * N, 2)], xp.at[pl.ds(y * N + 2, 2)]]
    onward_up, onward_down = remote(halves[0], halves[0], up, group(), 3), remote(halves[1], halves[1], down, group(), 4)
    turn = minus(zh, zl)

    @pl.when(root)
    def _():
        own_p.start()

    @otherwise(root)
    def _():
        collect.start()

    arrived(x_block(2), x_z[2])
    spread_x(2)
    arrived(a_block(0, 1), a_ring[0, 1])
    ring_a(0, 1, up, 2)
    spread_a(0, 1)
    arrived(a_block(1, 3), a_ring[1, 3])
    ring_a(1, 3, down, 2)
    send(xf, place, at(zl=zh, zh=plus(zh, 1)), from_below[0] + half)
    send(xf, place, at(zl=zh, zh=plus(zh, 3)), from_above[0] + half)
    spread_a(1, 3)
    arrived(a_block(0, 3), a_ring[0, 3])
    spread_a(0, 3)
    arrived(a_block(1, 1), a_ring[1, 1])
    spread_a(1, 1)
    share_x(0)
    send(kv.at[mine], kv.at[mine], mate, mate_k)

    for dx in DS:
        arrived(xq.at[pl.ds(minus(x, dx) * N, N), k], x_x[dx])
        share_x(dx)
    arrived(a_block(0, 2), a_ring[0, 2])
    spread_a(0, 2)
    arrived(a_block(1, 2), a_ring[1, 2])
    spread_a(1, 2)

    @pl.when(turn == 1)
    def _():
        arrived(halves[0], from_below[0])
        onward_up.start()

    @pl.when(turn == 3)
    def _():
        arrived(halves[1], from_above[1])
        onward_down.start()

    def project(p):
        acc = jnp.zeros((64, 256), F32)
        for dy in (0, *DS):
            ys = minus(y, dy) * N
            if dy:
                arrived(ag.at[p, pl.ds(ys, N)], a_y[p, dy])
            left = jnp.concatenate([ag[p, ys + h] for h in range(N)], axis=1)
            acc += dot(left, xq[pl.ds(ys, N)].reshape(512, 256), ((1,), (0,)))
        tg[p, R] = acc.astype(BF16)
        for d in DS:
            send(t_block(p, 0), t_block(p, 0), at(zl=plus(zl, d)), t_z[p, d])

    arrived(xq.at[:, 1 - k], x_k)
    project(0)
    spread_t(0, 0)
    project(1)
    spread_t(1, 0)
    for dz in DS:
        arrived(t_block(0, dz), t_z[0, dz])
        spread_t(0, dz)

    @pl.when(root)
    def _():
        own_p.wait()
        arrived(xp.at[pl.ds(0, 3)], f_z)

    @pl.when(turn == 1)
    def _():
        arrived(halves[1], from_below[1])

    @pl.when(turn == 3)
    def _():
        arrived(halves[0], from_above[0])

    @pl.when(turn == 2)
    def _():
        onward_up.wait_recv()
        onward_down.wait_recv()

    line = xp.at[pl.ds(y * N, N)]
    for d in DS:
        send(line, line, at(y=plus(y, d)), f_y)
    for dz in DS:
        arrived(t_block(1, dz), t_z[1, dz])
        spread_t(1, dz)
    relay_t(0)
    relay_t(1)
    arrived(xp.at[pl.ds(0, 12)], f_y)

    back = (*DS, 0)
    to_mate = {p: group() for p in range(2)}
    u_x = {(p, e): group() for p in range(2) for e in back}
    u_far = {(p, e): group() for p in range(2) for e in back}
    u_z = {p: group() for p in range(2)}
    o_y = {(p, e): group() for p in range(2) for e in back}
    o_z = {(p, e): group() for p in range(2) for e in DS}

    via = {0: 1, 3: 1, 1: 3, 2: 3}

    def pairs_part(p):
        acc = jnp.zeros((256, 256), F32)
        for dx in (0, *DS):
            xs = minus(x, dx) * N
            if dx:
                for dz, d in ((0, 3), (1, 1), (3, 3), (2, 1)):
                    if d == dx:
                        arrived(t_block(p, dz, d), t_x[p, d, dz])
                if dx == 2:
                    arrived(tg.at[p, pl.ds(xs, N)], t_far[p])
            left = xp[pl.ds(xs, N)].reshape(256, 256)
            right = tg[p, pl.ds(xs, N)].reshape(256, 256)
            acc += dot(left, right, ((0,), (0,)))
        gacc[p] = acc
        send(gacc.at[p], gr.at[p], mate, to_mate[p])

    def first_back(p):
        arrived(gr.at[p], to_mate[p])
        w = (kv[...] * (gacc[p] + gr[p])).astype(BF16)
        for dx in (*DS, 0):
            xs = plus(x, dx) * N
            part = dot(xp[pl.ds(xs, N)].reshape(256, 256), w, ((1,), (0,))).reshape(N, 64, 256)
            if dx:
                us[p, dx] = part.astype(BF16)
            else:
                us2[p] = part
        for e in back:
            send(us.at[p, 2, plus(zl, e)], urx.at[p, e, 2], at(x=plus(x, via[e])), u_far[p, e])
        for e in back:
            d = 4 - via[e]
            send(us.at[p, d, plus(zl, e)], urx.at[p, e, d], at(x=plus(x, d)), u_x[p, e])

    def relay_u(p):
        for e in back:
            d, h = via[e], plus(zl, e)
            arrived(urx.at[p, e, 2], u_far[p, e])
            us[p, d, h] = (us[p, d, h].astype(F32) + urx[p, e, 2].astype(F32)).astype(BF16)
            send(us.at[p, d, h], urx.at[p, e, d], at(x=plus(x, d)), u_x[p, e])

    def sum_x(p):
        for e in (*DS, 0):
            part = us2[p, plus(zl, e)]
            arrived(urx.at[p, e, pl.ds(0, 2)], u_x[p, e])
            for dx in (1, 3):
                part += urx[p, e, dx].astype(F32)
            if e:
                us[p, 0, e] = part.astype(BF16)
                send(us.at[p, 0, e], urz.at[p, e], at(zl=plus(zl, e)), u_z[p])
            else:
                us2[p, zl] = part

    def sum_z(p):
        part = us2[p, zl]
        arrived(urz.at[p, pl.ds(1, 3)], u_z[p])
        for e in DS:
            part += urz[p, e].astype(F32)
        u = part.astype(BF16)
        for dy in (*DS, 0):
            ys = plus(y, dy) * N
            part = dot(u, xq[pl.ds(ys, N)].reshape(512, 256), ((1,), (1,)))
            for h in range(N):
                piece = part[:, h * 128 : h * 128 + 128]
                if dy:
                    osd[p, dy, h] = piece.astype(BF16)
                else:
                    os2[p, h] = piece

    def spread_o(p, e):
        for dy in DS:
            place = osd.at[p, dy, plus(zh, e)]
            send(place, ory.at[p, e, dy], at(y=plus(y, dy)), o_y[p, e])

    def sum_y(p, e):
        part = os2[p, plus(zh, e)]
        arrived(ory.at[p, e, pl.ds(1, 3)], o_y[p, e])
        for dy in DS:
            part += ory[p, e, dy].astype(F32)
        if e == 2 or e == (3 if p == 0 else 1):
            osd[p, 0, e] = part.astype(BF16)
            ahead = p == 0 if e == 2 else e == 1
            send(osd.at[p, 0, e], orz.at[p, e], up if ahead else down, o_z[p, e])
        else:
            os2[p, plus(zh, e)] = part

    def pass_o(p):
        e = 1 if p == 0 else 3
        arrived(orz.at[p, 2], o_z[p, 2])
        osd[p, 0, e] = (os2[p, plus(zh, e)] + orz[p, 2].astype(F32)).astype(BF16)
        send(osd.at[p, 0, e], orz.at[p, e], up if e == 1 else down, o_z[p, e])

    def finish(p):
        part = os2[p, zh]
        for e in ((3, 1) if p == 0 else (1, 3)):
            arrived(orz.at[p, e], o_z[p, e])
            part += orz[p, e].astype(F32)
        out_ref[p] = part.astype(BF16)

    arrived(kv.at[theirs], mate_k)
    pairs_part(0)
    pairs_part(1)
    first_back(0)
    first_back(1)
    relay_u(0)
    relay_u(1)
    sum_x(0)
    sum_x(1)
    sum_z(0)
    spread_o(0, 2)
    spread_o(0, 1)
    sum_z(1)
    spread_o(1, 2)
    spread_o(1, 3)
    spread_o(0, 3)
    spread_o(1, 1)
    spread_o(0, 0)
    spread_o(1, 0)
    sum_y(0, 2)
    sum_y(0, 1)
    sum_y(1, 2)
    sum_y(1, 3)
    sum_y(0, 3)
    sum_y(1, 1)
    pass_o(0)
    pass_o(1)
    sum_y(0, 0)
    sum_y(1, 0)
    finish(0)
    finish(1)

    assert sent[0] == UNITS and used[0] <= COPIES, (sent[0], used[0])
    remote(all_sent, all_sent, mate, 0).wait_send()

    @otherwise(root)
    def _():
        collect.wait_send()

    @pl.when(turn == 1)
    def _():
        onward_up.wait_send()

    @pl.when(turn == 3)
    def _():
        onward_down.wait_send()


def per_device(amplitudes, factor, kern):
    any_spec = pl.BlockSpec(memory_space=pl.ANY)
    vmem = pltpu.VMEM
    dma = pltpu.SemaphoreType.DMA
    return pl.pallas_call(
        kernel,
        name="ladder",
        out_shape=pltpu.VMEM((2, 64, 128), BF16),
        in_specs=[any_spec] * 3,
        out_specs=pl.BlockSpec(memory_space=vmem),
        scratch_shapes=[
            vmem((256, 256), F32),
            vmem((2, 16, 64, 128), BF16),
            vmem((16, 2, 64, 256), BF16),
            vmem((64, 256), BF16),
            vmem((16, 64, 256), BF16),
            vmem((2, 16, 64, 256), BF16),
            vmem((2, 256, 256), F32),
            vmem((2, 256, 256), F32),
            vmem((2, 4, 4, 64, 256), BF16),
            vmem((2, 4, 4, 64, 256), BF16),
            vmem((2, 4, 64, 256), F32),
            vmem((2, 4, 64, 256), BF16),
            vmem((2, 4, 4, 64, 128), BF16),
            vmem((2, 4, 4, 64, 128), BF16),
            vmem((2, 4, 64, 128), F32),
            vmem((2, 4, 64, 128), BF16),
            vmem((UNITS, 64, 128), BF16),
            dma((5,)),
            dma((5,)),
            dma((COPIES,)),
        ],
        compiler_params=pltpu.CompilerParams(collective_id=0, has_side_effects=True),
    )(amplitudes, factor, kern)


def solution(mesh):
    placed = (P(None, "row", "col"), P("row", "col"), P("row", "col"))
    return jax.shard_map(
        per_device, mesh=mesh, in_specs=placed, out_specs=P(None, "row", "col"), check_vma=False
    )
```

```python
import math

import jax
import jax.numpy as jnp
from jax import lax
from jax.experimental import pallas as pl
from jax.experimental.pallas import tpu as pltpu
from jax.sharding import PartitionSpec as P

MESH = pl.DeviceIdType.MESH
F32, BF16 = jnp.float32, jnp.bfloat16
N = 4
DS = (1, 3, 2)
SUMS = ((0, 2), (0, 1), (1, 2), (1, 3), (0, 3), (1, 1), (0, 0), (1, 0))
COPIES = 71
UNIT = 64 * 128
UNITS = 310


def dot(a, b, dims):
    return lax.dot_general(a, b, (dims, ((), ())), preferred_element_type=F32)


def kernel(
    a_ref, x_ref, k_ref, out_ref,
    kv, ag, xq, xf, xp, tg, gacc, gr, us, urx, us2, urz, osd, ory, os2, orz, all_sent, lsem, ssem, rsem,
):
    row, col = lax.axis_index("row"), lax.axis_index("col")
    k = lax.rem(row, 2)
    R = lax.div(row, 2)
    x, zl = lax.div(R, N), lax.rem(R, N)
    y, zh = lax.div(col, N), lax.rem(col, N)
    C = col

    def at(x=x, zl=zl, k=k, y=y, zh=zh):
        return ((x * N + zl) * 2 + k, y * N + zh)

    def plus(v, d):
        return lax.rem(v + d, N)

    def minus(v, d):
        return lax.rem(v + N - d, N)

    mate = at(k=1 - k)
    flip = at(x=y, y=x)
    up, down = at(zh=plus(zh, 1)), at(zh=plus(zh, 3))
    swaps = x != y
    root = zl == zh

    used = [0]
    sent = [0]

    def group():
        used[0] += 1
        return used[0] - 1

    def remote(src, dst, device, number, mine=0):
        return pltpu.make_async_remote_copy(
            src_ref=src, dst_ref=dst, send_sem=ssem.at[mine], recv_sem=rsem.at[number],
            device_id=device, device_id_type=MESH,
        )

    def send(src, dst, device, number):
        remote(src, dst, device, number).start()
        sent[0] += math.prod(src.shape) * src.dtype.itemsize // 2 // UNIT

    def arrived(ref, number):
        remote(ref, ref, mate, number).wait_recv()

    def otherwise(condition):
        return pl.when(jnp.logical_not(condition))

    own_a = pltpu.make_async_copy(a_ref, ag.at[:, C], lsem.at[0])
    own_x = pltpu.make_async_copy(x_ref, xq.at[R, k], lsem.at[1])
    mine, theirs = pl.ds(k * 128, 128), pl.ds((1 - k) * 128, 128)
    own_k = pltpu.make_async_copy(k_ref, kv.at[mine], lsem.at[2])
    own_f = pltpu.make_async_copy(x_ref, xf, lsem.at[3])
    own_p = pltpu.make_async_copy(xf, xp.at[y * N + zl], lsem.at[4])
    for copy in (own_a, own_x, own_k):
        copy.start()

    barrier = pltpu.get_barrier_semaphore()
    partners = [up, down, mate]
    for d in DS:
        partners += [at(x=plus(x, d)), at(zl=plus(zl, d)), at(y=plus(y, d))]
    for device in partners:
        pl.semaphore_signal(barrier, inc=1, device_id=device, device_id_type=MESH)

    @pl.when(swaps)
    def _():
        pl.semaphore_signal(barrier, inc=1, device_id=flip, device_id_type=MESH)
        pl.semaphore_wait(barrier, len(partners) + 1)

    @otherwise(swaps)
    def _():
        own_f.start()
        pl.semaphore_wait(barrier, len(partners))

    own_a.wait()
    own_x.wait()
    own_k.wait()
    mate_k = group()

    def a_block(p, dz):
        return ag.at[p, y * N + minus(zh, dz)]

    def x_block(dz):
        return xq.at[x * N + minus(zl, dz), k]

    def t_block(p, dz, dx=0):
        return tg.at[p, minus(x, dx) * N + minus(zl, dz)]

    a_ring = {(p, dz): group() for p in range(2) for dz in DS}
    a_y = {(p, d): group() for p in range(2) for d in DS}
    x_z, x_x, x_k = {d: group() for d in DS}, {d: group() for d in DS}, group()
    t_z = {(p, d): group() for p in range(2) for d in DS}
    t_x = {(p, d): group() for p in range(2) for d in DS}
    f_x, f_z, f_y = group(), group(), group()

    def ring_a(p, dz, device, number):
        send(a_block(p, dz), a_block(p, dz), device, a_ring[p, number])

    def spread_a(p, dz):
        for d in DS:
            send(a_block(p, dz), a_block(p, dz), at(y=plus(y, d)), a_y[p, d])

    def spread_x(dz):
        for d in DS:
            send(x_block(dz), x_block(dz), at(x=plus(x, d)), x_x[d])

    def spread_t(p, dz):
        for d in DS:
            send(t_block(p, dz), t_block(p, dz), at(x=plus(x, d)), t_x[p, d])

    def share_x(dx):
        blocks = xq.at[pl.ds(minus(x, dx) * N, N), k]
        send(blocks, blocks, mate, x_k)

    ring_a(0, 0, up, 1)
    ring_a(1, 0, down, 3)
    for d in DS:
        send(x_block(0), x_block(0), at(zl=plus(zl, d)), x_z[d])
    ring_a(0, 0, down, 3)
    ring_a(1, 0, up, 1)
    flipped = remote(x_ref, xf, flip, f_x, 1)

    @pl.when(swaps)
    def _():
        flipped.start()

    spread_x(0)
    spread_a(0, 0)
    spread_a(1, 0)
    arrived(x_block(1), x_z[1])
    spread_x(1)
    arrived(x_block(3), x_z[3])
    spread_x(3)

    @pl.when(swaps)
    def _():
        flipped.wait_send()
        flipped.wait_recv()

    @otherwise(swaps)
    def _():
        own_f.wait()

    place = xp.at[y * N + zl]
    collect = remote(xf, place, at(zl=zh), f_z, 2)
    from_below, from_above = [group(), group()], [group(), group()]
    half = lax.div(zl, 2)
    halves = [xp.at[pl.ds(y * N, 2)], xp.at[pl.ds(y * N + 2, 2)]]
    onward_up, onward_down = remote(halves[0], halves[0], up, group(), 3), remote(halves[1], halves[1], down, group(), 4)
    turn = minus(zh, zl)

    @pl.when(root)
    def _():
        own_p.start()

    @otherwise(root)
    def _():
        collect.start()

    arrived(x_block(2), x_z[2])
    spread_x(2)
    arrived(a_block(0, 1), a_ring[0, 1])
    ring_a(0, 1, up, 2)
    spread_a(0, 1)
    arrived(a_block(1, 3), a_ring[1, 3])
    ring_a(1, 3, down, 2)
    send(xf, place, at(zl=zh, zh=plus(zh, 1)), from_below[0] + half)
    send(xf, place, at(zl=zh, zh=plus(zh, 3)), from_above[0] + half)
    spread_a(1, 3)
    arrived(a_block(0, 3), a_ring[0, 3])
    spread_a(0, 3)
    arrived(a_block(1, 1), a_ring[1, 1])
    spread_a(1, 1)
    share_x(0)
    send(kv.at[mine], kv.at[mine], mate, mate_k)

    for dx in DS:
        arrived(xq.at[pl.ds(minus(x, dx) * N, N), k], x_x[dx])
        share_x(dx)
    arrived(a_block(0, 2), a_ring[0, 2])
    spread_a(0, 2)
    arrived(a_block(1, 2), a_ring[1, 2])
    spread_a(1, 2)

    @pl.when(turn == 1)
    def _():
        arrived(halves[0], from_below[0])
        onward_up.start()

    @pl.when(turn == 3)
    def _():
        arrived(halves[1], from_above[1])
        onward_down.start()

    def project(p):
        acc = jnp.zeros((64, 256), F32)
        for dy in (0, *DS):
            ys = minus(y, dy) * N
            if dy:
                arrived(ag.at[p, pl.ds(ys, N)], a_y[p, dy])
            left = jnp.concatenate([ag[p, ys + h] for h in range(N)], axis=1)
            acc += dot(left, xq[pl.ds(ys, N)].reshape(512, 256), ((1,), (0,)))
        tg[p, R] = acc.astype(BF16)
        for d in DS:
            send(t_block(p, 0), t_block(p, 0), at(zl=plus(zl, d)), t_z[p, d])

    arrived(xq.at[:, 1 - k], x_k)
    project(0)
    spread_t(0, 0)
    project(1)
    spread_t(1, 0)
    for dz in DS:
        arrived(t_block(0, dz), t_z[0, dz])
        spread_t(0, dz)

    @pl.when(root)
    def _():
        own_p.wait()
        arrived(xp.at[pl.ds(0, 3)], f_z)

    @pl.when(turn == 1)
    def _():
        arrived(halves[1], from_below[1])

    @pl.when(turn == 3)
    def _():
        arrived(halves[0], from_above[0])

    @pl.when(turn == 2)
    def _():
        onward_up.wait_recv()
        onward_down.wait_recv()

    line = xp.at[pl.ds(y * N, N)]
    for d in DS:
        send(line, line, at(y=plus(y, d)), f_y)
    for dz in DS:
        arrived(t_block(1, dz), t_z[1, dz])
        spread_t(1, dz)
    arrived(xp.at[pl.ds(0, 12)], f_y)

    back = (*DS, 0)
    to_mate = {p: group() for p in range(2)}
    u_x = {(p, e): group() for p in range(2) for e in back}
    u_far = {(p, e): group() for p in range(2) for e in back}
    u_z = {p: group() for p in range(2)}
    o_y = {(p, e): group() for p in range(2) for e in back}
    o_z = {p: group() for p in range(2)}

    via = {0: 1, 3: 1, 1: 3, 2: 3}

    def pairs_part(p):
        acc = jnp.zeros((256, 256), F32)
        for dx in (0, *DS):
            xs = minus(x, dx) * N
            if dx:
                arrived(tg.at[p, pl.ds(xs, N)], t_x[p, dx])
            left = xp[pl.ds(xs, N)].reshape(256, 256)
            right = tg[p, pl.ds(xs, N)].reshape(256, 256)
            acc += dot(left, right, ((0,), (0,)))
        gacc[p] = acc
        send(gacc.at[p], gr.at[p], mate, to_mate[p])

    def first_back(p):
        arrived(gr.at[p], to_mate[p])
        w = (kv[...] * (gacc[p] + gr[p])).astype(BF16)
        for dx in (*DS, 0):
            xs = plus(x, dx) * N
            part = dot(xp[pl.ds(xs, N)].reshape(256, 256), w, ((1,), (0,))).reshape(N, 64, 256)
            if dx:
                us[p, dx] = part.astype(BF16)
            else:
                us2[p] = part
        for e in back:
            send(us.at[p, 2, plus(zl, e)], urx.at[p, e, 2], at(x=plus(x, via[e])), u_far[p, e])
        for e in back:
            d = 4 - via[e]
            send(us.at[p, d, plus(zl, e)], urx.at[p, e, d], at(x=plus(x, d)), u_x[p, e])

    def relay_u(p):
        for e in back:
            d, h = via[e], plus(zl, e)
            arrived(urx.at[p, e, 2], u_far[p, e])
            us[p, d, h] = (us[p, d, h].astype(F32) + urx[p, e, 2].astype(F32)).astype(BF16)
            send(us.at[p, d, h], urx.at[p, e, d], at(x=plus(x, d)), u_x[p, e])

    def sum_x(p):
        for e in (*DS, 0):
            part = us2[p, plus(zl, e)]
            arrived(urx.at[p, e, pl.ds(0, 2)], u_x[p, e])
            for dx in (1, 3):
                part += urx[p, e, dx].astype(F32)
            if e:
                us[p, 0, e] = part.astype(BF16)
                send(us.at[p, 0, e], urz.at[p, e], at(zl=plus(zl, e)), u_z[p])
            else:
                us2[p, zl] = part

    def sum_z(p):
        part = us2[p, zl]
        arrived(urz.at[p, pl.ds(1, 3)], u_z[p])
        for e in DS:
            part += urz[p, e].astype(F32)
        u = part.astype(BF16)
        for dy in (*DS, 0):
            ys = plus(y, dy) * N
            part = dot(u, xq[pl.ds(ys, N)].reshape(512, 256), ((1,), (1,)))
            for h in range(N):
                piece = part[:, h * 128 : h * 128 + 128]
                if dy:
                    osd[p, dy, h] = piece.astype(BF16)
                else:
                    os2[p, h] = piece

    def spread_o(p, e):
        for dy in DS:
            place = osd.at[p, dy, plus(zh, e)]
            send(place, ory.at[p, e, dy], at(y=plus(y, dy)), o_y[p, e])

    def sum_y(p, e):
        part = os2[p, plus(zh, e)]
        arrived(ory.at[p, e, pl.ds(1, 3)], o_y[p, e])
        for dy in DS:
            part += ory[p, e, dy].astype(F32)
        if e:
            osd[p, 0, e] = part.astype(BF16)
            send(osd.at[p, 0, e], orz.at[p, e], at(zh=plus(zh, e)), o_z[p])
        else:
            os2[p, zh] = part

    def finish(p):
        part = os2[p, zh]
        arrived(orz.at[p, pl.ds(1, 3)], o_z[p])
        for e in DS:
            part += orz[p, e].astype(F32)
        out_ref[p] = part.astype(BF16)

    arrived(kv.at[theirs], mate_k)
    pairs_part(0)
    pairs_part(1)
    first_back(0)
    first_back(1)
    relay_u(0)
    relay_u(1)
    sum_x(0)
    sum_x(1)
    sum_z(0)
    spread_o(0, 2)
    spread_o(0, 1)
    sum_z(1)
    for p, e in SUMS[2:]:
        spread_o(p, e)
    for p, e in SUMS:
        sum_y(p, e)
    finish(0)
    finish(1)

    assert sent[0] == UNITS and used[0] <= COPIES, (sent[0], used[0])
    remote(all_sent, all_sent, mate, 0).wait_send()

    @otherwise(root)
    def _():
        collect.wait_send()

    @pl.when(turn == 1)
    def _():
        onward_up.wait_send()

    @pl.when(turn == 3)
    def _():
        onward_down.wait_send()


def per_device(amplitudes, factor, kern):
    any_spec = pl.BlockSpec(memory_space=pl.ANY)
    vmem = pltpu.VMEM
    dma = pltpu.SemaphoreType.DMA
    return pl.pallas_call(
        kernel,
        name="ladder",
        out_shape=pltpu.VMEM((2, 64, 128), BF16),
        in_specs=[any_spec] * 3,
        out_specs=pl.BlockSpec(memory_space=vmem),
        scratch_shapes=[
            vmem((256, 256), F32),
            vmem((2, 16, 64, 128), BF16),
            vmem((16, 2, 64, 256), BF16),
            vmem((64, 256), BF16),
            vmem((16, 64, 256), BF16),
            vmem((2, 16, 64, 256), BF16),
            vmem((2, 256, 256), F32),
            vmem((2, 256, 256), F32),
            vmem((2, 4, 4, 64, 256), BF16),
            vmem((2, 4, 4, 64, 256), BF16),
            vmem((2, 4, 64, 256), F32),
            vmem((2, 4, 64, 256), BF16),
            vmem((2, 4, 4, 64, 128), BF16),
            vmem((2, 4, 4, 64, 128), BF16),
            vmem((2, 4, 64, 128), F32),
            vmem((2, 4, 64, 128), BF16),
            vmem((UNITS, 64, 128), BF16),
            dma((5,)),
            dma((5,)),
            dma((COPIES,)),
        ],
        compiler_params=pltpu.CompilerParams(collective_id=0, has_side_effects=True),
    )(amplitudes, factor, kern)


def solution(mesh):
    placed = (P(None, "row", "col"), P("row", "col"), P("row", "col"))
    return jax.shard_map(
        per_device, mesh=mesh, in_specs=placed, out_specs=P(None, "row", "col"), check_vma=False
    )
```

```python
import math

import jax
import jax.numpy as jnp
from jax import lax
from jax.experimental import pallas as pl
from jax.experimental.pallas import tpu as pltpu
from jax.sharding import PartitionSpec as P

MESH = pl.DeviceIdType.MESH
F32, BF16 = jnp.float32, jnp.bfloat16
N = 4
DS = (1, 3, 2)
SUMS = ((0, 2), (0, 1), (1, 2), (1, 3), (0, 3), (1, 1), (0, 0), (1, 0))
COPIES = 71
UNIT = 64 * 128
UNITS = 310


def dot(a, b, dims):
    return lax.dot_general(a, b, (dims, ((), ())), preferred_element_type=F32)


def kernel(
    a_ref, x_ref, k_ref, out_ref,
    kv, ag, xq, xf, xp, tg, gacc, gr, us, urx, us2, urz, osd, ory, os2, orz, all_sent, lsem, ssem, rsem,
):
    row, col = lax.axis_index("row"), lax.axis_index("col")
    k = lax.rem(row, 2)
    R = lax.div(row, 2)
    x, zl = lax.div(R, N), lax.rem(R, N)
    y, zh = lax.div(col, N), lax.rem(col, N)
    C = col

    def at(x=x, zl=zl, k=k, y=y, zh=zh):
        return ((x * N + zl) * 2 + k, y * N + zh)

    def plus(v, d):
        return lax.rem(v + d, N)

    def minus(v, d):
        return lax.rem(v + N - d, N)

    mate = at(k=1 - k)
    flip = at(x=y, y=x)
    up, down = at(zh=plus(zh, 1)), at(zh=plus(zh, 3))
    swaps = x != y
    root = zl == zh

    used = [0]
    sent = [0]

    def group():
        used[0] += 1
        return used[0] - 1

    def remote(src, dst, device, number, mine=0):
        return pltpu.make_async_remote_copy(
            src_ref=src, dst_ref=dst, send_sem=ssem.at[mine], recv_sem=rsem.at[number],
            device_id=device, device_id_type=MESH,
        )

    def send(src, dst, device, number):
        remote(src, dst, device, number).start()
        sent[0] += math.prod(src.shape) * src.dtype.itemsize // 2 // UNIT

    def arrived(ref, number):
        remote(ref, ref, mate, number).wait_recv()

    def otherwise(condition):
        return pl.when(jnp.logical_not(condition))

    own_a = pltpu.make_async_copy(a_ref, ag.at[:, C], lsem.at[0])
    own_x = pltpu.make_async_copy(x_ref, xq.at[R, k], lsem.at[1])
    mine, theirs = pl.ds(k * 128, 128), pl.ds((1 - k) * 128, 128)
    own_k = pltpu.make_async_copy(k_ref, kv.at[mine], lsem.at[2])
    own_f = pltpu.make_async_copy(x_ref, xf, lsem.at[3])
    own_p = pltpu.make_async_copy(xf, xp.at[y * N + zl], lsem.at[4])
    for copy in (own_a, own_x, own_k):
        copy.start()

    barrier = pltpu.get_barrier_semaphore()
    partners = [up, down, mate]
    for d in DS:
        partners += [at(x=plus(x, d)), at(zl=plus(zl, d)), at(y=plus(y, d))]
    for device in partners:
        pl.semaphore_signal(barrier, inc=1, device_id=device, device_id_type=MESH)

    @pl.when(swaps)
    def _():
        pl.semaphore_signal(barrier, inc=1, device_id=flip, device_id_type=MESH)
        pl.semaphore_wait(barrier, len(partners) + 1)

    @otherwise(swaps)
    def _():
        own_f.start()
        pl.semaphore_wait(barrier, len(partners))

    own_a.wait()
    own_x.wait()
    own_k.wait()
    mate_k = group()

    def a_block(p, dz):
        return ag.at[p, y * N + minus(zh, dz)]

    def x_block(dz):
        return xq.at[x * N + minus(zl, dz), k]

    def t_block(p, dz, dx=0):
        return tg.at[p, minus(x, dx) * N + minus(zl, dz)]

    a_ring = {(p, dz): group() for p in range(2) for dz in DS}
    a_y = {(p, d): group() for p in range(2) for d in DS}
    x_z, x_x, x_k = {d: group() for d in DS}, {d: group() for d in DS}, group()
    t_z = {(p, d): group() for p in range(2) for d in DS}
    t_x = {(p, d): group() for p in range(2) for d in DS}
    f_x, f_z, f_y = group(), group(), group()

    def ring_a(p, dz, device, number):
        send(a_block(p, dz), a_block(p, dz), device, a_ring[p, number])

    def spread_a(p, dz):
        for d in DS:
            send(a_block(p, dz), a_block(p, dz), at(y=plus(y, d)), a_y[p, d])

    def spread_x(dz):
        for d in DS:
            send(x_block(dz), x_block(dz), at(x=plus(x, d)), x_x[d])

    def spread_t(p, dz):
        for d in DS:
            send(t_block(p, dz), t_block(p, dz), at(x=plus(x, d)), t_x[p, d])

    def share_x(dx):
        blocks = xq.at[pl.ds(minus(x, dx) * N, N), k]
        send(blocks, blocks, mate, x_k)

    ring_a(0, 0, up, 1)
    ring_a(1, 0, down, 3)
    ring_a(0, 0, down, 3)
    ring_a(1, 0, up, 1)
    for d in DS:
        send(x_block(0), x_block(0), at(zl=plus(zl, d)), x_z[d])
    flipped = remote(x_ref, xf, flip, f_x, 1)

    @pl.when(swaps)
    def _():
        flipped.start()

    spread_x(0)
    spread_a(0, 0)
    spread_a(1, 0)
    arrived(x_block(1), x_z[1])
    spread_x(1)
    arrived(x_block(3), x_z[3])
    spread_x(3)

    @pl.when(swaps)
    def _():
        flipped.wait_send()
        flipped.wait_recv()

    @otherwise(swaps)
    def _():
        own_f.wait()

    place = xp.at[y * N + zl]
    collect = remote(xf, place, at(zl=zh), f_z, 2)
    from_below, from_above = [group(), group()], [group(), group()]
    half = lax.div(zl, 2)
    halves = [xp.at[pl.ds(y * N, 2)], xp.at[pl.ds(y * N + 2, 2)]]
    onward_up, onward_down = remote(halves[0], halves[0], up, group(), 3), remote(halves[1], halves[1], down, group(), 4)
    turn = minus(zh, zl)

    @pl.when(root)
    def _():
        own_p.start()

    @otherwise(root)
    def _():
        collect.start()

    arrived(x_block(2), x_z[2])
    spread_x(2)
    arrived(a_block(0, 1), a_ring[0, 1])
    ring_a(0, 1, up, 2)
    spread_a(0, 1)
    arrived(a_block(1, 3), a_ring[1, 3])
    ring_a(1, 3, down, 2)
    send(xf, place, at(zl=zh, zh=plus(zh, 1)), from_below[0] + half)
    send(xf, place, at(zl=zh, zh=plus(zh, 3)), from_above[0] + half)
    spread_a(1, 3)
    arrived(a_block(0, 3), a_ring[0, 3])
    spread_a(0, 3)
    arrived(a_block(1, 1), a_ring[1, 1])
    spread_a(1, 1)
    share_x(0)
    send(kv.at[mine], kv.at[mine], mate, mate_k)

    for dx in DS:
        arrived(xq.at[pl.ds(minus(x, dx) * N, N), k], x_x[dx])
        share_x(dx)
    arrived(a_block(0, 2), a_ring[0, 2])
    spread_a(0, 2)
    arrived(a_block(1, 2), a_ring[1, 2])
    spread_a(1, 2)

    line = xp.at[pl.ds(y * N, N)]

    def spread_p(blocks):
        for d in DS:
            remote(blocks, blocks, at(y=plus(y, d)), f_y).start()

    sent[0] += 3 * math.prod(line.shape) // UNIT

    @pl.when(root)
    def _():
        own_p.wait()
        arrived(xp.at[pl.ds(0, 3)], f_z)
        spread_p(line)

    @pl.when(turn == 1)
    def _():
        arrived(halves[0], from_below[0])
        onward_up.start()

    @pl.when(turn == 3)
    def _():
        arrived(halves[1], from_above[1])
        onward_down.start()

    def project(p):
        acc = jnp.zeros((64, 256), F32)
        for dy in (0, *DS):
            ys = minus(y, dy) * N
            if dy:
                arrived(ag.at[p, pl.ds(ys, N)], a_y[p, dy])
            left = jnp.concatenate([ag[p, ys + h] for h in range(N)], axis=1)
            acc += dot(left, xq[pl.ds(ys, N)].reshape(512, 256), ((1,), (0,)))
        tg[p, R] = acc.astype(BF16)
        for d in DS:
            send(t_block(p, 0), t_block(p, 0), at(zl=plus(zl, d)), t_z[p, d])

    arrived(xq.at[:, 1 - k], x_k)
    project(0)
    spread_t(0, 0)

    @pl.when(turn == 1)
    def _():
        arrived(halves[1], from_below[1])
        spread_p(line)

    @pl.when(turn == 3)
    def _():
        arrived(halves[0], from_above[0])
        spread_p(line)

    project(1)
    spread_t(1, 0)
    for dz in DS:
        arrived(t_block(0, dz), t_z[0, dz])
        spread_t(0, dz)
        if dz == 1:
            @pl.when(turn == 2)
            def _():
                onward_up.wait_recv()
                spread_p(halves[0])
                onward_down.wait_recv()
                spread_p(halves[1])

    for dz in DS:
        arrived(t_block(1, dz), t_z[1, dz])
        spread_t(1, dz)
    arrived(xp.at[pl.ds(0, 12)], f_y)

    back = (*DS, 0)
    to_mate = {p: group() for p in range(2)}
    u_x = {(p, e): group() for p in range(2) for e in back}
    u_far = {(p, e): group() for p in range(2) for e in back}
    u_z = {p: group() for p in range(2)}
    o_y = {(p, e): group() for p in range(2) for e in back}
    o_z = {p: group() for p in range(2)}

    via = {0: 1, 3: 1, 1: 3, 2: 3}

    def pairs_part(p):
        acc = jnp.zeros((256, 256), F32)
        for dx in (0, *DS):
            xs = minus(x, dx) * N
            if dx:
                arrived(tg.at[p, pl.ds(xs, N)], t_x[p, dx])
            left = xp[pl.ds(xs, N)].reshape(256, 256)
            right = tg[p, pl.ds(xs, N)].reshape(256, 256)
            acc += dot(left, right, ((0,), (0,)))
        gacc[p] = acc
        send(gacc.at[p], gr.at[p], mate, to_mate[p])

    def first_back(p):
        arrived(gr.at[p], to_mate[p])
        w = (kv[...] * (gacc[p] + gr[p])).astype(BF16)
        for dx in (*DS, 0):
            xs = plus(x, dx) * N
            part = dot(xp[pl.ds(xs, N)].reshape(256, 256), w, ((1,), (0,))).reshape(N, 64, 256)
            if dx:
                us[p, dx] = part.astype(BF16)
            else:
                us2[p] = part
        for e in back:
            send(us.at[p, 2, plus(zl, e)], urx.at[p, e, 2], at(x=plus(x, via[e])), u_far[p, e])
        for e in back:
            d = 4 - via[e]
            send(us.at[p, d, plus(zl, e)], urx.at[p, e, d], at(x=plus(x, d)), u_x[p, e])

    def relay_u(p):
        for e in back:
            d, h = via[e], plus(zl, e)
            arrived(urx.at[p, e, 2], u_far[p, e])
            us[p, d, h] = (us[p, d, h].astype(F32) + urx[p, e, 2].astype(F32)).astype(BF16)
            send(us.at[p, d, h], urx.at[p, e, d], at(x=plus(x, d)), u_x[p, e])

    def sum_x(p):
        for e in (*DS, 0):
            part = us2[p, plus(zl, e)]
            arrived(urx.at[p, e, pl.ds(0, 2)], u_x[p, e])
            for dx in (1, 3):
                part += urx[p, e, dx].astype(F32)
            if e:
                us[p, 0, e] = part.astype(BF16)
                send(us.at[p, 0, e], urz.at[p, e], at(zl=plus(zl, e)), u_z[p])
            else:
                us2[p, zl] = part

    def sum_z(p):
        part = us2[p, zl]
        arrived(urz.at[p, pl.ds(1, 3)], u_z[p])
        for e in DS:
            part += urz[p, e].astype(F32)
        u = part.astype(BF16)
        for dy in (*DS, 0):
            ys = plus(y, dy) * N
            part = dot(u, xq[pl.ds(ys, N)].reshape(512, 256), ((1,), (1,)))
            for h in range(N):
                piece = part[:, h * 128 : h * 128 + 128]
                if dy:
                    osd[p, dy, h] = piece.astype(BF16)
                else:
                    os2[p, h] = piece

    def spread_o(p, e):
        for dy in DS:
            place = osd.at[p, dy, plus(zh, e)]
            send(place, ory.at[p, e, dy], at(y=plus(y, dy)), o_y[p, e])

    def sum_y(p, e):
        part = os2[p, plus(zh, e)]
        arrived(ory.at[p, e, pl.ds(1, 3)], o_y[p, e])
        for dy in DS:
            part += ory[p, e, dy].astype(F32)
        if e:
            osd[p, 0, e] = part.astype(BF16)
            send(osd.at[p, 0, e], orz.at[p, e], at(zh=plus(zh, e)), o_z[p])
        else:
            os2[p, zh] = part

    def finish(p):
        part = os2[p, zh]
        arrived(orz.at[p, pl.ds(1, 3)], o_z[p])
        for e in DS:
            part += orz[p, e].astype(F32)
        out_ref[p] = part.astype(BF16)

    arrived(kv.at[theirs], mate_k)
    pairs_part(0)
    pairs_part(1)
    first_back(0)
    first_back(1)
    relay_u(0)
    relay_u(1)
    sum_x(0)
    sum_x(1)
    sum_z(0)
    spread_o(0, 2)
    spread_o(0, 1)
    sum_z(1)
    for p, e in SUMS[2:]:
        spread_o(p, e)
    for p, e in SUMS:
        sum_y(p, e)
    finish(0)
    finish(1)

    assert sent[0] == UNITS and used[0] <= COPIES, (sent[0], used[0])
    remote(all_sent, all_sent, mate, 0).wait_send()

    @otherwise(root)
    def _():
        collect.wait_send()

    @pl.when(turn == 1)
    def _():
        onward_up.wait_send()

    @pl.when(turn == 3)
    def _():
        onward_down.wait_send()


def per_device(amplitudes, factor, kern):
    any_spec = pl.BlockSpec(memory_space=pl.ANY)
    vmem = pltpu.VMEM
    dma = pltpu.SemaphoreType.DMA
    return pl.pallas_call(
        kernel,
        name="ladder",
        out_shape=pltpu.VMEM((2, 64, 128), BF16),
        in_specs=[any_spec] * 3,
        out_specs=pl.BlockSpec(memory_space=vmem),
        scratch_shapes=[
            vmem((256, 256), F32),
            vmem((2, 16, 64, 128), BF16),
            vmem((16, 2, 64, 256), BF16),
            vmem((64, 256), BF16),
            vmem((16, 64, 256), BF16),
            vmem((2, 16, 64, 256), BF16),
            vmem((2, 256, 256), F32),
            vmem((2, 256, 256), F32),
            vmem((2, 4, 4, 64, 256), BF16),
            vmem((2, 4, 4, 64, 256), BF16),
            vmem((2, 4, 64, 256), F32),
            vmem((2, 4, 64, 256), BF16),
            vmem((2, 4, 4, 64, 128), BF16),
            vmem((2, 4, 4, 64, 128), BF16),
            vmem((2, 4, 64, 128), F32),
            vmem((2, 4, 64, 128), BF16),
            vmem((UNITS, 64, 128), BF16),
            dma((5,)),
            dma((5,)),
            dma((COPIES,)),
        ],
        compiler_params=pltpu.CompilerParams(collective_id=0, has_side_effects=True),
    )(amplitudes, factor, kern)


def solution(mesh):
    placed = (P(None, "row", "col"), P("row", "col"), P("row", "col"))
    return jax.shard_map(
        per_device, mesh=mesh, in_specs=placed, out_specs=P(None, "row", "col"), check_vma=False
    )
```

```python
import math

import jax
import jax.numpy as jnp
from jax import lax
from jax.experimental import pallas as pl
from jax.experimental.pallas import tpu as pltpu
from jax.sharding import PartitionSpec as P

MESH = pl.DeviceIdType.MESH
F32, BF16 = jnp.float32, jnp.bfloat16
N = 4
DS = (1, 3, 2)
SUMS = ((0, 2), (0, 1), (1, 2), (1, 3), (0, 3), (1, 1), (0, 0), (1, 0))
COPIES = 71
UNIT = 64 * 128
UNITS = 310


def dot(a, b, dims):
    return lax.dot_general(a, b, (dims, ((), ())), preferred_element_type=F32)


def kernel(
    a_ref, x_ref, k_ref, out_ref,
    kv, ag, xq, xf, xp, tg, gacc, gr, us, urx, us2, urz, osd, ory, os2, orz, all_sent, lsem, ssem, rsem,
):
    row, col = lax.axis_index("row"), lax.axis_index("col")
    k = lax.rem(row, 2)
    R = lax.div(row, 2)
    x, zl = lax.div(R, N), lax.rem(R, N)
    y, zh = lax.div(col, N), lax.rem(col, N)
    C = col

    def at(x=x, zl=zl, k=k, y=y, zh=zh):
        return ((x * N + zl) * 2 + k, y * N + zh)

    def plus(v, d):
        return lax.rem(v + d, N)

    def minus(v, d):
        return lax.rem(v + N - d, N)

    mate = at(k=1 - k)
    flip = at(x=y, y=x)
    up, down = at(zh=plus(zh, 1)), at(zh=plus(zh, 3))
    swaps = x != y
    root = zl == zh

    used = [0]
    sent = [0]

    def group():
        used[0] += 1
        return used[0] - 1

    def remote(src, dst, device, number, mine=0):
        return pltpu.make_async_remote_copy(
            src_ref=src, dst_ref=dst, send_sem=ssem.at[mine], recv_sem=rsem.at[number],
            device_id=device, device_id_type=MESH,
        )

    def send(src, dst, device, number):
        remote(src, dst, device, number).start()
        sent[0] += math.prod(src.shape) * src.dtype.itemsize // 2 // UNIT

    def arrived(ref, number):
        remote(ref, ref, mate, number).wait_recv()

    def otherwise(condition):
        return pl.when(jnp.logical_not(condition))

    own_a = pltpu.make_async_copy(a_ref, ag.at[:, C], lsem.at[0])
    own_x = pltpu.make_async_copy(x_ref, xq.at[R, k], lsem.at[1])
    mine, theirs = pl.ds(k * 128, 128), pl.ds((1 - k) * 128, 128)
    own_k = pltpu.make_async_copy(k_ref, kv.at[mine], lsem.at[2])
    own_f = pltpu.make_async_copy(x_ref, xf, lsem.at[3])
    own_p = pltpu.make_async_copy(xf, xp.at[y * N + zl], lsem.at[4])
    for copy in (own_a, own_x, own_k):
        copy.start()

    barrier = pltpu.get_barrier_semaphore()
    partners = [up, down, mate]
    for d in DS:
        partners += [at(x=plus(x, d)), at(zl=plus(zl, d)), at(y=plus(y, d))]
    for device in partners:
        pl.semaphore_signal(barrier, inc=1, device_id=device, device_id_type=MESH)

    @pl.when(swaps)
    def _():
        pl.semaphore_signal(barrier, inc=1, device_id=flip, device_id_type=MESH)
        pl.semaphore_wait(barrier, len(partners) + 1)

    @otherwise(swaps)
    def _():
        own_f.start()
        pl.semaphore_wait(barrier, len(partners))

    own_a.wait()
    own_x.wait()
    own_k.wait()
    mate_k = group()

    def a_block(p, dz):
        return ag.at[p, y * N + minus(zh, dz)]

    def x_block(dz):
        return xq.at[x * N + minus(zl, dz), k]

    def t_block(p, dz, dx=0):
        return tg.at[p, minus(x, dx) * N + minus(zl, dz)]

    a_ring = {(p, dz): group() for p in range(2) for dz in DS}
    a_y = {(p, d): group() for p in range(2) for d in DS}
    x_z, x_x, x_k = {d: group() for d in DS}, {d: group() for d in DS}, group()
    t_z = {(p, d): group() for p in range(2) for d in DS}
    t_x = {(p, d): group() for p in range(2) for d in DS}
    f_x, f_z, f_y = group(), group(), group()

    def ring_a(p, dz, device, number):
        send(a_block(p, dz), a_block(p, dz), device, a_ring[p, number])

    def spread_a(p, dz):
        for d in DS:
            send(a_block(p, dz), a_block(p, dz), at(y=plus(y, d)), a_y[p, d])

    def spread_x(dz):
        send(x_block(dz), x_block(dz), mate, x_k)
        for d in DS:
            send(x_block(dz), x_block(dz), at(x=plus(x, d)), x_x[d])

    def spread_t(p, dz):
        for d in DS:
            send(t_block(p, dz), t_block(p, dz), at(x=plus(x, d)), t_x[p, d])

    def share_x(dx):
        blocks = xq.at[pl.ds(minus(x, dx) * N, N), k]
        send(blocks, blocks, mate, x_k)

    ring_a(0, 0, up, 1)
    ring_a(1, 0, down, 3)
    ring_a(0, 0, down, 3)
    ring_a(1, 0, up, 1)
    for d in DS:
        send(x_block(0), x_block(0), at(zl=plus(zl, d)), x_z[d])
    flipped = remote(x_ref, xf, flip, f_x, 1)

    @pl.when(swaps)
    def _():
        flipped.start()

    spread_x(0)
    spread_a(0, 0)
    spread_a(1, 0)
    arrived(x_block(1), x_z[1])
    spread_x(1)
    arrived(x_block(3), x_z[3])
    spread_x(3)

    @pl.when(swaps)
    def _():
        flipped.wait_send()
        flipped.wait_recv()

    @otherwise(swaps)
    def _():
        own_f.wait()

    place = xp.at[y * N + zl]
    collect = remote(xf, place, at(zl=zh), f_z, 2)
    from_below, from_above = [group(), group()], [group(), group()]
    half = lax.div(zl, 2)
    halves = [xp.at[pl.ds(y * N, 2)], xp.at[pl.ds(y * N + 2, 2)]]
    onward_up, onward_down = remote(halves[0], halves[0], up, group(), 3), remote(halves[1], halves[1], down, group(), 4)
    turn = minus(zh, zl)

    @pl.when(root)
    def _():
        own_p.start()

    @otherwise(root)
    def _():
        collect.start()

    arrived(x_block(2), x_z[2])
    spread_x(2)
    arrived(a_block(0, 1), a_ring[0, 1])
    ring_a(0, 1, up, 2)
    spread_a(0, 1)
    arrived(a_block(1, 3), a_ring[1, 3])
    ring_a(1, 3, down, 2)
    send(xf, place, at(zl=zh, zh=plus(zh, 1)), from_below[0] + half)
    send(xf, place, at(zl=zh, zh=plus(zh, 3)), from_above[0] + half)
    spread_a(1, 3)
    arrived(a_block(0, 3), a_ring[0, 3])
    spread_a(0, 3)
    arrived(a_block(1, 1), a_ring[1, 1])
    spread_a(1, 1)
    send(kv.at[mine], kv.at[mine], mate, mate_k)

    for dx in DS:
        arrived(xq.at[pl.ds(minus(x, dx) * N, N), k], x_x[dx])
        share_x(dx)
    arrived(a_block(0, 2), a_ring[0, 2])
    spread_a(0, 2)
    arrived(a_block(1, 2), a_ring[1, 2])
    spread_a(1, 2)

    line = xp.at[pl.ds(y * N, N)]

    def spread_p(blocks):
        for d in DS:
            remote(blocks, blocks, at(y=plus(y, d)), f_y).start()

    sent[0] += 3 * math.prod(line.shape) // UNIT

    @pl.when(root)
    def _():
        own_p.wait()
        arrived(xp.at[pl.ds(0, 3)], f_z)
        spread_p(line)

    @pl.when(turn == 1)
    def _():
        arrived(halves[0], from_below[0])
        onward_up.start()

    @pl.when(turn == 3)
    def _():
        arrived(halves[1], from_above[1])
        onward_down.start()

    def project(p):
        acc = jnp.zeros((64, 256), F32)
        for dy in (0, *DS):
            ys = minus(y, dy) * N
            if dy:
                arrived(ag.at[p, pl.ds(ys, N)], a_y[p, dy])
            left = jnp.concatenate([ag[p, ys + h] for h in range(N)], axis=1)
            acc += dot(left, xq[pl.ds(ys, N)].reshape(512, 256), ((1,), (0,)))
        tg[p, R] = acc.astype(BF16)
        for d in DS:
            send(t_block(p, 0), t_block(p, 0), at(zl=plus(zl, d)), t_z[p, d])

    arrived(xq.at[:, 1 - k], x_k)
    project(0)
    spread_t(0, 0)

    @pl.when(turn == 1)
    def _():
        arrived(halves[1], from_below[1])
        spread_p(line)

    @pl.when(turn == 3)
    def _():
        arrived(halves[0], from_above[0])
        spread_p(line)

    project(1)
    spread_t(1, 0)
    for dz in DS:
        arrived(t_block(0, dz), t_z[0, dz])
        spread_t(0, dz)
        if dz == 1:
            @pl.when(turn == 2)
            def _():
                onward_up.wait_recv()
                spread_p(halves[0])
                onward_down.wait_recv()
                spread_p(halves[1])

    for dz in DS:
        arrived(t_block(1, dz), t_z[1, dz])
        spread_t(1, dz)
    arrived(xp.at[pl.ds(0, 12)], f_y)

    back = (*DS, 0)
    to_mate = {p: group() for p in range(2)}
    u_x = {(p, e): group() for p in range(2) for e in back}
    u_far = {(p, e): group() for p in range(2) for e in back}
    u_z = {p: group() for p in range(2)}
    o_y = {(p, e): group() for p in range(2) for e in back}
    o_z = {p: group() for p in range(2)}

    via = {0: 1, 3: 1, 1: 3, 2: 3}

    def pairs_part(p):
        acc = jnp.zeros((256, 256), F32)
        for dx in (0, *DS):
            xs = minus(x, dx) * N
            if dx:
                arrived(tg.at[p, pl.ds(xs, N)], t_x[p, dx])
            left = xp[pl.ds(xs, N)].reshape(256, 256)
            right = tg[p, pl.ds(xs, N)].reshape(256, 256)
            acc += dot(left, right, ((0,), (0,)))
        gacc[p] = acc
        send(gacc.at[p], gr.at[p], mate, to_mate[p])

    def first_back(p):
        arrived(gr.at[p], to_mate[p])
        w = (kv[...] * (gacc[p] + gr[p])).astype(BF16)
        for dx in (2, 1, 3, 0):
            xs = plus(x, dx) * N
            part = dot(xp[pl.ds(xs, N)].reshape(256, 256), w, ((1,), (0,))).reshape(N, 64, 256)
            if dx == 0:
                us2[p] = part
                continue
            us[p, dx] = part.astype(BF16)
            for e in back:
                block = us.at[p, dx, plus(zl, e)]
                if dx == 2:
                    send(block, urx.at[p, e, 2], at(x=plus(x, via[e])), u_far[p, e])
                elif dx != via[e]:
                    send(block, urx.at[p, e, dx], at(x=plus(x, dx)), u_x[p, e])

    def relay_u(p):
        for e in back:
            d, h = via[e], plus(zl, e)
            arrived(urx.at[p, e, 2], u_far[p, e])
            us[p, d, h] = (us[p, d, h].astype(F32) + urx[p, e, 2].astype(F32)).astype(BF16)
            send(us.at[p, d, h], urx.at[p, e, d], at(x=plus(x, d)), u_x[p, e])

    def sum_x(p):
        for e in (*DS, 0):
            part = us2[p, plus(zl, e)]
            arrived(urx.at[p, e, pl.ds(0, 2)], u_x[p, e])
            for dx in (1, 3):
                part += urx[p, e, dx].astype(F32)
            if e:
                us[p, 0, e] = part.astype(BF16)
                send(us.at[p, 0, e], urz.at[p, e], at(zl=plus(zl, e)), u_z[p])
            else:
                us2[p, zl] = part

    def sum_z(p):
        part = us2[p, zl]
        arrived(urz.at[p, pl.ds(1, 3)], u_z[p])
        for e in DS:
            part += urz[p, e].astype(F32)
        u = part.astype(BF16)
        for dy in (*DS, 0):
            ys = plus(y, dy) * N
            part = dot(u, xq[pl.ds(ys, N)].reshape(512, 256), ((1,), (1,)))
            for h in range(N):
                piece = part[:, h * 128 : h * 128 + 128]
                if dy:
                    osd[p, dy, h] = piece.astype(BF16)
                else:
                    os2[p, h] = piece

    def spread_o(p, e):
        for dy in DS:
            place = osd.at[p, dy, plus(zh, e)]
            send(place, ory.at[p, e, dy], at(y=plus(y, dy)), o_y[p, e])

    def sum_y(p, e):
        part = os2[p, plus(zh, e)]
        arrived(ory.at[p, e, pl.ds(1, 3)], o_y[p, e])
        for dy in DS:
            part += ory[p, e, dy].astype(F32)
        if e:
            osd[p, 0, e] = part.astype(BF16)
            send(osd.at[p, 0, e], orz.at[p, e], at(zh=plus(zh, e)), o_z[p])
        else:
            os2[p, zh] = part

    def finish(p):
        part = os2[p, zh]
        arrived(orz.at[p, pl.ds(1, 3)], o_z[p])
        for e in DS:
            part += orz[p, e].astype(F32)
        out_ref[p] = part.astype(BF16)

    arrived(kv.at[theirs], mate_k)
    pairs_part(0)
    pairs_part(1)
    first_back(0)
    first_back(1)
    relay_u(0)
    relay_u(1)
    sum_x(0)
    sum_x(1)
    sum_z(0)
    spread_o(0, 2)
    spread_o(0, 1)
    sum_z(1)
    for p, e in SUMS[2:]:
        spread_o(p, e)
    for p, e in SUMS:
        sum_y(p, e)
    finish(0)
    finish(1)

    assert sent[0] == UNITS and used[0] <= COPIES, (sent[0], used[0])
    remote(all_sent, all_sent, mate, 0).wait_send()

    @otherwise(root)
    def _():
        collect.wait_send()

    @pl.when(turn == 1)
    def _():
        onward_up.wait_send()

    @pl.when(turn == 3)
    def _():
        onward_down.wait_send()


def per_device(amplitudes, factor, kern):
    any_spec = pl.BlockSpec(memory_space=pl.ANY)
    vmem = pltpu.VMEM
    dma = pltpu.SemaphoreType.DMA
    return pl.pallas_call(
        kernel,
        name="ladder",
        out_shape=pltpu.VMEM((2, 64, 128), BF16),
        in_specs=[any_spec] * 3,
        out_specs=pl.BlockSpec(memory_space=vmem),
        scratch_shapes=[
            vmem((256, 256), F32),
            vmem((2, 16, 64, 128), BF16),
            vmem((16, 2, 64, 256), BF16),
            vmem((64, 256), BF16),
            vmem((16, 64, 256), BF16),
            vmem((2, 16, 64, 256), BF16),
            vmem((2, 256, 256), F32),
            vmem((2, 256, 256), F32),
            vmem((2, 4, 4, 64, 256), BF16),
            vmem((2, 4, 4, 64, 256), BF16),
            vmem((2, 4, 64, 256), F32),
            vmem((2, 4, 64, 256), BF16),
            vmem((2, 4, 4, 64, 128), BF16),
            vmem((2, 4, 4, 64, 128), BF16),
            vmem((2, 4, 64, 128), F32),
            vmem((2, 4, 64, 128), BF16),
            vmem((UNITS, 64, 128), BF16),
            dma((5,)),
            dma((5,)),
            dma((COPIES,)),
        ],
        compiler_params=pltpu.CompilerParams(collective_id=0, has_side_effects=True),
    )(amplitudes, factor, kern)


def solution(mesh):
    placed = (P(None, "row", "col"), P("row", "col"), P("row", "col"))
    return jax.shard_map(
        per_device, mesh=mesh, in_specs=placed, out_specs=P(None, "row", "col"), check_vma=False
    )
```

```python
import math

import jax
import jax.numpy as jnp
from jax import lax
from jax.experimental import pallas as pl
from jax.experimental.pallas import tpu as pltpu
from jax.sharding import PartitionSpec as P

MESH = pl.DeviceIdType.MESH
F32, BF16 = jnp.float32, jnp.bfloat16
N = 4
DS = (1, 3, 2)
SUMS = ((0, 2), (0, 1), (1, 2), (1, 3), (0, 3), (1, 1), (0, 0), (1, 0))
COPIES = 71
UNIT = 64 * 128
UNITS = 310


def dot(a, b, dims):
    return lax.dot_general(a, b, (dims, ((), ())), preferred_element_type=F32)


def kernel(
    a_ref, x_ref, k_ref, out_ref,
    kv, ag, xq, xf, xp, tg, gacc, gr, us, urx, us2, urz, osd, ory, os2, orz, all_sent, lsem, ssem, rsem,
):
    row, col = lax.axis_index("row"), lax.axis_index("col")
    k = lax.rem(row, 2)
    R = lax.div(row, 2)
    x, zl = lax.div(R, N), lax.rem(R, N)
    y, zh = lax.div(col, N), lax.rem(col, N)
    C = col

    def at(x=x, zl=zl, k=k, y=y, zh=zh):
        return ((x * N + zl) * 2 + k, y * N + zh)

    def plus(v, d):
        return lax.rem(v + d, N)

    def minus(v, d):
        return lax.rem(v + N - d, N)

    mate = at(k=1 - k)
    flip = at(x=y, y=x)
    up, down = at(zh=plus(zh, 1)), at(zh=plus(zh, 3))
    swaps = x != y
    root = zl == zh

    used = [0]
    sent = [0]

    def group():
        used[0] += 1
        return used[0] - 1

    def remote(src, dst, device, number, mine=0):
        return pltpu.make_async_remote_copy(
            src_ref=src, dst_ref=dst, send_sem=ssem.at[mine], recv_sem=rsem.at[number],
            device_id=device, device_id_type=MESH,
        )

    def send(src, dst, device, number):
        remote(src, dst, device, number).start()
        sent[0] += math.prod(src.shape) * src.dtype.itemsize // 2 // UNIT

    def arrived(ref, number):
        remote(ref, ref, mate, number).wait_recv()

    def otherwise(condition):
        return pl.when(jnp.logical_not(condition))

    own_a = pltpu.make_async_copy(a_ref, ag.at[:, C], lsem.at[0])
    own_x = pltpu.make_async_copy(x_ref, xq.at[R, k], lsem.at[1])
    mine, theirs = pl.ds(k * 128, 128), pl.ds((1 - k) * 128, 128)
    own_k = pltpu.make_async_copy(k_ref, kv.at[mine], lsem.at[2])
    own_f = pltpu.make_async_copy(x_ref, xf, lsem.at[3])
    own_p = pltpu.make_async_copy(xf, xp.at[y * N + zl], lsem.at[4])
    for copy in (own_a, own_x, own_k):
        copy.start()

    barrier = pltpu.get_barrier_semaphore()
    partners = [up, down, mate]
    for d in DS:
        partners += [at(x=plus(x, d)), at(zl=plus(zl, d)), at(y=plus(y, d))]
    for device in partners:
        pl.semaphore_signal(barrier, inc=1, device_id=device, device_id_type=MESH)

    @pl.when(swaps)
    def _():
        pl.semaphore_signal(barrier, inc=1, device_id=flip, device_id_type=MESH)
        pl.semaphore_wait(barrier, len(partners) + 1)

    @otherwise(swaps)
    def _():
        own_f.start()
        pl.semaphore_wait(barrier, len(partners))

    own_a.wait()
    own_x.wait()
    own_k.wait()
    mate_k = group()

    def a_block(p, dz):
        return ag.at[p, y * N + minus(zh, dz)]

    def x_block(dz):
        return xq.at[x * N + minus(zl, dz), k]

    def t_block(p, dz, dx=0):
        return tg.at[p, minus(x, dx) * N + minus(zl, dz)]

    a_ring = {(p, dz): group() for p in range(2) for dz in DS}
    a_y = {(p, d): group() for p in range(2) for d in DS}
    x_z, x_x, x_k = {d: group() for d in DS}, {d: group() for d in DS}, group()
    t_z = {(p, d): group() for p in range(2) for d in DS}
    t_x = {(p, d): group() for p in range(2) for d in DS}
    f_x, f_z, f_y = group(), group(), group()

    def ring_a(p, dz, device, number):
        send(a_block(p, dz), a_block(p, dz), device, a_ring[p, number])

    def spread_a(p, dz):
        for d in DS:
            send(a_block(p, dz), a_block(p, dz), at(y=plus(y, d)), a_y[p, d])

    def spread_x(dz):
        send(x_block(dz), x_block(dz), mate, x_k)
        for d in DS:
            send(x_block(dz), x_block(dz), at(x=plus(x, d)), x_x[d])

    def spread_t(p, dz):
        for d in DS:
            send(t_block(p, dz), t_block(p, dz), at(x=plus(x, d)), t_x[p, d])

    def share_x(dx):
        blocks = xq.at[pl.ds(minus(x, dx) * N, N), k]
        send(blocks, blocks, mate, x_k)

    ring_a(0, 0, up, 1)
    ring_a(1, 0, down, 3)
    ring_a(0, 0, down, 3)
    ring_a(1, 0, up, 1)
    for d in DS:
        send(x_block(0), x_block(0), at(zl=plus(zl, d)), x_z[d])
    flipped = remote(x_ref, xf, flip, f_x, 1)

    @pl.when(swaps)
    def _():
        flipped.start()

    spread_x(0)
    spread_a(0, 0)
    spread_a(1, 0)
    arrived(x_block(1), x_z[1])
    spread_x(1)
    arrived(a_block(0, 1), a_ring[0, 1])
    ring_a(0, 1, up, 2)
    spread_a(0, 1)
    arrived(a_block(1, 3), a_ring[1, 3])
    ring_a(1, 3, down, 2)
    arrived(x_block(3), x_z[3])
    spread_x(3)

    @pl.when(swaps)
    def _():
        flipped.wait_send()
        flipped.wait_recv()

    @otherwise(swaps)
    def _():
        own_f.wait()

    place = xp.at[y * N + zl]
    collect = remote(xf, place, at(zl=zh), f_z, 2)
    from_below, from_above = [group(), group()], [group(), group()]
    half = lax.div(zl, 2)
    halves = [xp.at[pl.ds(y * N, 2)], xp.at[pl.ds(y * N + 2, 2)]]
    onward_up, onward_down = remote(halves[0], halves[0], up, group(), 3), remote(halves[1], halves[1], down, group(), 4)
    turn = minus(zh, zl)

    @pl.when(root)
    def _():
        own_p.start()

    @otherwise(root)
    def _():
        collect.start()

    arrived(x_block(2), x_z[2])
    spread_x(2)
    send(xf, place, at(zl=zh, zh=plus(zh, 1)), from_below[0] + half)
    send(xf, place, at(zl=zh, zh=plus(zh, 3)), from_above[0] + half)
    spread_a(1, 3)
    arrived(a_block(0, 3), a_ring[0, 3])
    spread_a(0, 3)
    arrived(a_block(1, 1), a_ring[1, 1])
    spread_a(1, 1)
    send(kv.at[mine], kv.at[mine], mate, mate_k)

    for dx in DS:
        arrived(xq.at[pl.ds(minus(x, dx) * N, N), k], x_x[dx])
        share_x(dx)
    arrived(a_block(0, 2), a_ring[0, 2])
    spread_a(0, 2)
    arrived(a_block(1, 2), a_ring[1, 2])
    spread_a(1, 2)

    line = xp.at[pl.ds(y * N, N)]

    def spread_p(blocks):
        for d in DS:
            remote(blocks, blocks, at(y=plus(y, d)), f_y).start()

    sent[0] += 3 * math.prod(line.shape) // UNIT

    @pl.when(root)
    def _():
        own_p.wait()
        arrived(xp.at[pl.ds(0, 3)], f_z)
        spread_p(line)

    @pl.when(turn == 1)
    def _():
        arrived(halves[0], from_below[0])
        onward_up.start()

    @pl.when(turn == 3)
    def _():
        arrived(halves[1], from_above[1])
        onward_down.start()

    def project(p):
        acc = jnp.zeros((64, 256), F32)
        for dy in (0, *DS):
            ys = minus(y, dy) * N
            if dy:
                arrived(ag.at[p, pl.ds(ys, N)], a_y[p, dy])
            left = jnp.concatenate([ag[p, ys + h] for h in range(N)], axis=1)
            acc += dot(left, xq[pl.ds(ys, N)].reshape(512, 256), ((1,), (0,)))
        tg[p, R] = acc.astype(BF16)
        for d in DS:
            send(t_block(p, 0), t_block(p, 0), at(zl=plus(zl, d)), t_z[p, d])

    arrived(xq.at[:, 1 - k], x_k)
    project(0)
    spread_t(0, 0)

    @pl.when(turn == 1)
    def _():
        arrived(halves[1], from_below[1])
        spread_p(line)

    @pl.when(turn == 3)
    def _():
        arrived(halves[0], from_above[0])
        spread_p(line)

    project(1)
    spread_t(1, 0)
    for dz in DS:
        arrived(t_block(0, dz), t_z[0, dz])
        spread_t(0, dz)
        if dz == 1:
            @pl.when(turn == 2)
            def _():
                onward_up.wait_recv()
                spread_p(halves[0])
                onward_down.wait_recv()
                spread_p(halves[1])

    for dz in DS:
        arrived(t_block(1, dz), t_z[1, dz])
        spread_t(1, dz)
    arrived(xp.at[pl.ds(0, 12)], f_y)

    back = (*DS, 0)
    to_mate = {p: group() for p in range(2)}
    u_x = {(p, e): group() for p in range(2) for e in back}
    u_far = {(p, e): group() for p in range(2) for e in back}
    u_z = {p: group() for p in range(2)}
    o_y = {(p, e): group() for p in range(2) for e in back}
    o_z = {p: group() for p in range(2)}

    via = {0: 1, 3: 1, 1: 3, 2: 3}

    def pairs_part(p):
        acc = jnp.zeros((256, 256), F32)
        for dx in (0, *DS):
            xs = minus(x, dx) * N
            if dx:
                arrived(tg.at[p, pl.ds(xs, N)], t_x[p, dx])
            left = xp[pl.ds(xs, N)].reshape(256, 256)
            right = tg[p, pl.ds(xs, N)].reshape(256, 256)
            acc += dot(left, right, ((0,), (0,)))
        gacc[p] = acc
        send(gacc.at[p], gr.at[p], mate, to_mate[p])

    def first_back(p):
        arrived(gr.at[p], to_mate[p])
        w = (kv[...] * (gacc[p] + gr[p])).astype(BF16)
        for dx in (2, 1, 3, 0):
            xs = plus(x, dx) * N
            part = dot(xp[pl.ds(xs, N)].reshape(256, 256), w, ((1,), (0,))).reshape(N, 64, 256)
            if dx == 0:
                us2[p] = part
                continue
            us[p, dx] = part.astype(BF16)
            for e in back:
                block = us.at[p, dx, plus(zl, e)]
                if dx == 2:
                    send(block, urx.at[p, e, 2], at(x=plus(x, via[e])), u_far[p, e])
                elif dx != via[e]:
                    send(block, urx.at[p, e, dx], at(x=plus(x, dx)), u_x[p, e])

    def relay_u(p):
        for e in back:
            d, h = via[e], plus(zl, e)
            arrived(urx.at[p, e, 2], u_far[p, e])
            us[p, d, h] = (us[p, d, h].astype(F32) + urx[p, e, 2].astype(F32)).astype(BF16)
            send(us.at[p, d, h], urx.at[p, e, d], at(x=plus(x, d)), u_x[p, e])

    def sum_x(p):
        for e in (*DS, 0):
            part = us2[p, plus(zl, e)]
            arrived(urx.at[p, e, pl.ds(0, 2)], u_x[p, e])
            for dx in (1, 3):
                part += urx[p, e, dx].astype(F32)
            if e:
                us[p, 0, e] = part.astype(BF16)
                send(us.at[p, 0, e], urz.at[p, e], at(zl=plus(zl, e)), u_z[p])
            else:
                us2[p, zl] = part

    def send_o(p, e, dy):
        place = osd.at[p, dy, plus(zh, e)]
        send(place, ory.at[p, e, dy], at(y=plus(y, dy)), o_y[p, e])

    def sum_z(p):
        part = us2[p, zl]
        arrived(urz.at[p, pl.ds(1, 3)], u_z[p])
        for e in DS:
            part += urz[p, e].astype(F32)
        u = part.astype(BF16)
        for dy in (*DS, 0):
            ys = plus(y, dy) * N
            part = dot(u, xq[pl.ds(ys, N)].reshape(512, 256), ((1,), (1,)))
            for h in range(N):
                piece = part[:, h * 128 : h * 128 + 128]
                if dy:
                    osd[p, dy, h] = piece.astype(BF16)
                else:
                    os2[p, h] = piece
            if dy:
                send_o(p, 2, dy)

    def spread_o(p, e):
        for dy in DS:
            send_o(p, e, dy)

    def sum_y(p, e):
        part = os2[p, plus(zh, e)]
        arrived(ory.at[p, e, pl.ds(1, 3)], o_y[p, e])
        for dy in DS:
            part += ory[p, e, dy].astype(F32)
        if e:
            osd[p, 0, e] = part.astype(BF16)
            send(osd.at[p, 0, e], orz.at[p, e], at(zh=plus(zh, e)), o_z[p])
        else:
            os2[p, zh] = part

    def finish(p):
        part = os2[p, zh]
        arrived(orz.at[p, pl.ds(1, 3)], o_z[p])
        for e in DS:
            part += orz[p, e].astype(F32)
        out_ref[p] = part.astype(BF16)

    arrived(kv.at[theirs], mate_k)
    pairs_part(0)
    pairs_part(1)
    first_back(0)
    first_back(1)
    relay_u(0)
    relay_u(1)
    sum_x(0)
    sum_x(1)
    sum_z(0)
    spread_o(0, 1)
    sum_z(1)
    for p, e in SUMS[3:]:
        spread_o(p, e)
    for p, e in SUMS:
        sum_y(p, e)
    finish(0)
    finish(1)

    assert sent[0] == UNITS and used[0] <= COPIES, (sent[0], used[0])
    remote(all_sent, all_sent, mate, 0).wait_send()

    @otherwise(root)
    def _():
        collect.wait_send()

    @pl.when(turn == 1)
    def _():
        onward_up.wait_send()

    @pl.when(turn == 3)
    def _():
        onward_down.wait_send()


def per_device(amplitudes, factor, kern):
    any_spec = pl.BlockSpec(memory_space=pl.ANY)
    vmem = pltpu.VMEM
    dma = pltpu.SemaphoreType.DMA
    return pl.pallas_call(
        kernel,
        name="ladder",
        out_shape=pltpu.VMEM((2, 64, 128), BF16),
        in_specs=[any_spec] * 3,
        out_specs=pl.BlockSpec(memory_space=vmem),
        scratch_shapes=[
            vmem((256, 256), F32),
            vmem((2, 16, 64, 128), BF16),
            vmem((16, 2, 64, 256), BF16),
            vmem((64, 256), BF16),
            vmem((16, 64, 256), BF16),
            vmem((2, 16, 64, 256), BF16),
            vmem((2, 256, 256), F32),
            vmem((2, 256, 256), F32),
            vmem((2, 4, 4, 64, 256), BF16),
            vmem((2, 4, 4, 64, 256), BF16),
            vmem((2, 4, 64, 256), F32),
            vmem((2, 4, 64, 256), BF16),
            vmem((2, 4, 4, 64, 128), BF16),
            vmem((2, 4, 4, 64, 128), BF16),
            vmem((2, 4, 64, 128), F32),
            vmem((2, 4, 64, 128), BF16),
            vmem((UNITS, 64, 128), BF16),
            dma((5,)),
            dma((5,)),
            dma((COPIES,)),
        ],
        compiler_params=pltpu.CompilerParams(collective_id=0, has_side_effects=True),
    )(amplitudes, factor, kern)


def solution(mesh):
    placed = (P(None, "row", "col"), P("row", "col"), P("row", "col"))
    return jax.shard_map(
        per_device, mesh=mesh, in_specs=placed, out_specs=P(None, "row", "col"), check_vma=False
    )
```
